256 devices in a mesh: energy: 64 (over x, z_hi, y), space: 4 (over z_lo, core).
Axes of the slice: x: 4, y: 4, z: 8 (z_hi: 4, z_lo: 2; z = z_hi * 2 + z_lo), core: 2. Of those that a mesh axis runs over, the one named last changes fastest.
Arguments:
- g_lesser: bfloat16 [64, 2, 4, 512, 512], P('energy', None, 'space'), may hold values from -6 to 6, as said below
- w_lesser: bfloat16 [64, 2, 4, 512, 512], P('energy', None, 'space'), may hold values from -6 to 6, as said below
- g_retarded: bfloat16 [64, 2, 4, 4, 512, 512], P('energy', None, 'space'), may hold values from -0.1875 to 0.1875
- energy_index: int32 [64], replicated, may hold values from 0 to 63, each once
Outputs:
- sigma_lesser: bfloat16 [64, 2, 4, 512, 512], P('energy', None, 'space')
- delta_green: bfloat16 [64, 2, 4, 512, 512], P('energy', None, 'space')
The draws below stay inside these ranges and needn't reach their ends.
Inputs may be any that keep to these rules, and one draw needn't show every extreme that they name: `g_lesser`: anti-Hermitian in every diagonal block at every energy: element (j, i) of component 0 is minus element (i, j), of component 1 equal to it. `w_lesser`: anti-Hermitian in every diagonal block at every energy: element (j, i) of component 0 is minus element (i, j), of component 1 equal to it. `energy_index`: each grid point once.
All inputs are finite; a program needn't handle non-finite values.
Results may differ from the reference program's by a relative error of at most 0.013.
Values may be sent and summed in bfloat16 or wider, within the bound.
A program may use at most 128 MiB of HBM per device.

```python
import jax
import jax.numpy as jnp
from jax import lax

B = 512
NE = 64
NB = 4


def anti_hermitian(key):
    first_key, second_key = jax.random.split(key, 2)
    block_shape = (NE, NB, B, B)
    noise_real = jax.random.normal(first_key, block_shape, jnp.float32)
    noise_imag = jax.random.normal(second_key, block_shape, jnp.float32)
    real_part = (noise_real - jnp.swapaxes(noise_real, -1, -2)) * 0.70710678
    imag_part = (noise_imag + jnp.swapaxes(noise_imag, -1, -2)) * 0.70710678
    stacked = jnp.stack([real_part, imag_part], axis=1)
    return jnp.clip(stacked, -6.0, 6.0).astype(jnp.bfloat16)


def draw_g_lesser(key, part):
    return anti_hermitian(jax.random.fold_in(key, 11))


def draw_w_lesser(key, part):
    return anti_hermitian(jax.random.fold_in(key, 23))


def shard_levels(key, shape, cuts, low, high):
    level = 1.0
    for dim, parts in cuts:
        draws = jax.random.uniform(jax.random.fold_in(jax.random.fold_in(key, 6), dim), (parts,), jnp.float32, low / len(cuts), high / len(cuts))
        level = level * jnp.repeat(jnp.exp(draws), shape[dim] // parts).reshape((-1,) + (1,) * (len(shape) - 1 - dim))
    return level


def bell_draw(own_key, extent, deviation, reach, shards=(), held_as=jnp.bfloat16):
    factor_of = shard_levels(own_key, extent, shards, -0.22, 0.18) if shards else 1.0
    drawn = jax.random.normal(own_key, extent, jnp.float32) * deviation * factor_of
    return jnp.minimum(jnp.maximum(drawn, -reach), reach).astype(held_as)


def setup_inputs(seed: int = 0) -> dict:
    streams_of = jax.random.split(jax.random.key(seed), 5)
    return {
        "g_lesser": draw_g_lesser(jax.random.fold_in(streams_of[4], 71), 0),
        "w_lesser": draw_w_lesser(jax.random.fold_in(streams_of[4], 71), 0),
        "g_retarded": bell_draw(streams_of[2], (NE, 2, NB, NB, B, B), (2 * B) ** -0.5, 0.1875, ((0, 64), (2, 4))),
        "energy_index": jax.random.permutation(streams_of[3], NE).astype(jnp.int32),
    }


def convolve_block(operands):
    green, screen = operands
    green_c = green[:, 0].astype(jnp.float32) + 1j * green[:, 1].astype(jnp.float32)
    screen_c = screen[:, 0].astype(jnp.float32) + 1j * screen[:, 1].astype(jnp.float32)
    green_hat = jnp.fft.fft(green_c, n=2 * NE, axis=0)
    screen_hat = jnp.fft.fft(screen_c, n=2 * NE, axis=0)
    product = jnp.fft.ifft(green_hat * screen_hat, axis=0)[NE // 2:NE // 2 + NE]
    sigma_c = 1j * (NE ** -0.5) * product
    return jnp.stack([jnp.real(sigma_c), jnp.imag(sigma_c)], axis=1).astype(jnp.bfloat16)


def two_sided(operands):
    sigma_e, retarded = operands
    sig_real = sigma_e[0].astype(jnp.float32)
    sig_imag = sigma_e[1].astype(jnp.float32)
    ret_real = retarded[0].astype(jnp.float32)
    ret_imag = retarded[1].astype(jnp.float32)
    left_real = jnp.einsum('skij,kjl->skil', ret_real, sig_real) - jnp.einsum('skij,kjl->skil', ret_imag, sig_imag)
    left_imag = jnp.einsum('skij,kjl->skil', ret_real, sig_imag) + jnp.einsum('skij,kjl->skil', ret_imag, sig_real)
    left_real = lax.optimization_barrier(left_real.astype(jnp.bfloat16)).astype(jnp.float32)
    left_imag = lax.optimization_barrier(left_imag.astype(jnp.bfloat16)).astype(jnp.float32)
    out_real = jnp.einsum('skil,skml->sim', left_real, ret_real) + jnp.einsum('skil,skml->sim', left_imag, ret_imag)
    out_imag = jnp.einsum('skil,skml->sim', left_imag, ret_real) - jnp.einsum('skil,skml->sim', left_real, ret_imag)
    return jnp.stack([out_real, out_imag], axis=0).astype(jnp.bfloat16)


def reference(g_lesser, w_lesser, g_retarded, energy_index):
    to_grid = jnp.argsort(energy_index).astype(jnp.int32)
    green_grid = jnp.moveaxis(g_lesser[to_grid], 2, 0)
    screen_grid = jnp.moveaxis(w_lesser[to_grid], 2, 0)
    sigma_grid = lax.map(convolve_block, (green_grid, screen_grid))
    sigma_lesser = jnp.moveaxis(sigma_grid, 0, 2)[energy_index.astype(jnp.int32)]
    delta_green = lax.map(two_sided, (sigma_lesser, g_retarded))
    return sigma_lesser, delta_green
```

```python
import functools
import math

import jax
import jax.numpy as jnp
import numpy as np
from jax import lax
from jax.experimental import pallas as pl
from jax.experimental.pallas import tpu as pltpu
from jax.sharding import PartitionSpec as P

MESH = pl.DeviceIdType.MESH
NE = 64
B = 512
T = 128
LEN = 96
CHUNKS = 2
TILES = (((0, 0), (0, 1), (0, 2), (1, 2)), ((2, 2), (0, 3), (1, 3), (2, 3)))
BF = jnp.bfloat16
F32 = jnp.float32


def tables():
    f = np.arange(LEN)[:, None]
    p = np.arange(NE)[None, :]
    ang = 2 * math.pi * ((f * p) % LEN) / LEN
    c, s = np.cos(ang), np.sin(ang)
    forward = np.block([[c, s], [-s, c]])
    ang = 2 * math.pi * ((f * (p + NE // 2)) % LEN) / LEN
    c, s = np.cos(ang).T, np.sin(ang).T
    backward = np.block([[-s, -c], [c, -s]]) * (NE**-0.5 / LEN)

    def halves(m):
        m = m.astype(np.float32)
        hi = m.astype(jnp.bfloat16)
        lo = (m - hi.astype(np.float32)).astype(jnp.bfloat16)
        return np.stack([hi, lo])

    twice = np.concatenate([np.eye(NE), np.eye(NE)], axis=1).astype(jnp.bfloat16)
    return halves(forward), halves(backward), twice


def mm(a, b):
    return jnp.dot(a, b, preferred_element_type=F32)


def iotas(n=T):
    return lax.broadcasted_iota(jnp.int32, (n, n), 0), lax.broadcasted_iota(jnp.int32, (n, n), 1)


def body(g_hbm, w_hbm, r_hbm, idx_ref, ft_ref, bt_ref, tw_ref, sig_ref, del_ref,
         g_v, w_v, r_v, rt_v, send, recv, ssend, u_v, scr, xb, ph, pl_, fm, bm, um0, um1, xr, xi,
         lsem, gws, gwr, sgs, sgr, gas, gar):
    me = lax.axis_index("energy")
    sp = lax.axis_index("space")
    sp_core = sp // 2 * 2 + (sp + 1) % 2
    sp_z = (sp + 2) % 4
    sp_zc = (sp_core + 2) % 4

    cg = pltpu.make_async_copy(g_hbm, g_v, lsem.at[0])
    cw = pltpu.make_async_copy(w_hbm, w_v, lsem.at[1])
    cr = pltpu.make_async_copy(r_hbm, r_v, lsem.at[2])
    cg.start()
    cw.start()
    cr.start()

    barrier = pltpu.get_barrier_semaphore()

    @pl.loop(1, NE)
    def _(i):
        pl.semaphore_signal(barrier, inc=1, device_id=((me + i) % NE, sp), device_id_type=MESH)

    pl.semaphore_signal(barrier, inc=1, device_id=(me, sp_core), device_id_type=MESH)
    pl.semaphore_signal(barrier, inc=1, device_id=(me, sp_z), device_id_type=MESH)

    row, col = iotas()
    cg.wait()
    cw.wait()
    for h in range(CHUNKS):
        for t, (i, j) in enumerate(TILES[h]):
            dst = pl.ds(16 * t, 16)
            for a, src in enumerate((g_v, w_v)):
                if i == j:
                    d0r = src[0, T * i:T * i + T, T * i:T * i + T].astype(F32)
                    d0i = src[1, T * i:T * i + T, T * i:T * i + T].astype(F32)
                    k = i + 1
                    d1r = src[0, T * k:T * k + T, T * k:T * k + T].astype(F32)
                    d1i = src[1, T * k:T * k + T, T * k:T * k + T].astype(F32)
                    pr = jnp.where(row < col, d0r, jnp.where(row > col, d1r, d1i))
                    pi = jnp.where(row <= col, d0i, d1i)
                    send[h, dst, a, 0] = pr.reshape(16, 8, T).astype(BF)
                    send[h, dst, a, 1] = pi.reshape(16, 8, T).astype(BF)
                else:
                    for c in range(2):
                        blk = src[c, T * i:T * i + T, T * j:T * j + T].astype(F32)
                        send[h, dst, a, c] = blk.reshape(16, 8, T).astype(BF)

    pl.semaphore_wait(barrier, NE + 1)

    for h in range(CHUNKS):
        @pl.loop(1, NE)
        def _(i):
            d = (me + i) % NE
            pltpu.make_async_remote_copy(
                src_ref=send.at[h, d], dst_ref=recv.at[h, me], send_sem=gws.at[h], recv_sem=gwr.at[h],
                device_id=(d, sp), device_id_type=MESH).start()

        pltpu.make_async_copy(send.at[h, me], recv.at[h, me], gwr.at[h]).start()

    idx = jnp.broadcast_to(idx_ref[...].astype(F32), (8, NE)).astype(BF)
    both = mm(idx, tw_ref[...])[0:1, :]
    point = (row % NE).astype(F32)
    pick = jnp.where((point == both) & (row // NE == col // NE), 1.0, 0.0).astype(BF)
    for a in range(2):
        fm[a] = mm(ft_ref[a], pick).astype(BF)
        bm[a] = lax.dot_general(pick, bt_ref[a], (((0,), (0,)), ((), ())), preferred_element_type=F32).astype(BF)

    zero = jnp.zeros((T, T), BF)
    for c in range(2):
        um0[c, T:, :T] = zero
        um1[c, 3 * T:, :T] = zero
    xr[...] = jnp.zeros_like(xr)
    xi[...] = jnp.zeros_like(xi)
    cr.wait()

    @pl.loop(0, 8)
    def _(q):
        for i in range(4):
            for j in range(4):
                blk = r_v[q, T * i:T * i + T, T * j:T * j + T].astype(F32)
                rt_v[q, T * j:T * j + T, T * i:T * i + T] = blk.T.astype(BF)

    lane8 = lax.broadcasted_iota(jnp.int32, (T, T), 1)
    base = me % 16 * 8
    for h in range(CHUNKS):
        pltpu.make_async_copy(recv.at[h], recv.at[h], gwr.at[h]).wait()
        for a in range(2):
            for c in range(2):
                blk = recv[h, :, a, c].astype(F32)
                scr[a, c * 512:c * 512 + 512, :] = blk.reshape(512, T)
        for a in range(2):
            diag = jnp.zeros((T, T), F32)
            for i in range(8):
                x_i = scr[a, pl.ds(i, T, stride=8), :]
                diag = jnp.where(lane8 == base + i, x_i, diag)
                xb[a, :, T * i:T * i + T] = x_i.astype(BF)
            xb[a, :, 8 * T:9 * T] = jnp.where(row < NE, diag, 0.0).astype(BF)
            xb[a, :, 9 * T:] = jnp.where(row < NE, 0.0, diag).astype(BF)
        for n in range(5):
            cols = slice(256 * n, 256 * n + 256)
            gx = xb[0, :, cols]
            wx = xb[1, :, cols]
            gh = mm(fm[0], gx) + mm(fm[1], gx)
            wh = mm(fm[0], wx) + mm(fm[1], wx)
            pr = gh[:LEN] * wh[:LEN] - gh[LEN:] * wh[LEN:]
            pi = gh[:LEN] * wh[LEN:] + gh[LEN:] * wh[:LEN]
            prod = jnp.concatenate([pr, pi], axis=0)
            hi = prod.astype(BF)
            ph[:, cols] = hi
            pl_[:, cols] = (prod - hi.astype(F32)).astype(BF)
        tail = slice(8 * T, 10 * T)
        y = mm(bm[0], ph[:, tail]) + mm(bm[1], ph[:, tail]) + mm(bm[0], pl_[:, tail])
        fix = jnp.concatenate([-y[NE:, :T], y[NE:, T:]], axis=0)
        for n in range(4):
            cols = slice(256 * n, 256 * n + 256)
            y = mm(bm[0], ph[:, cols]) + mm(bm[1], ph[:, cols]) + mm(bm[0], pl_[:, cols])
            for m in range(2):
                i = 2 * n + m
                hit = (lane8 == base + i) & (me < 16)
                scr[0, pl.ds(i, T, stride=8), :] = jnp.where(hit, fix, y[:, T * m:T * m + T])
        for c in range(2):
            ssend[h, :, c] = scr[0, c * 512:c * 512 + 512, :].reshape(NE, 8, T).astype(BF)

        @pl.loop(1, NE)
        def _(i):
            d = (me + i) % NE
            pltpu.make_async_remote_copy(
                src_ref=ssend.at[h, d], dst_ref=u_v.at[sp, h, :, me], send_sem=sgs.at[h], recv_sem=sgr.at[h],
                device_id=(d, sp), device_id_type=MESH).start()

        pltpu.make_async_copy(ssend.at[h, me], u_v.at[sp, h, :, me], sgr.at[h]).start()

    def hop(k, h, lane, to):
        return pltpu.make_async_remote_copy(
            src_ref=u_v.at[k, h], dst_ref=u_v.at[k, h], send_sem=gas.at[h, lane], recv_sem=gar.at[h, lane],
            device_id=(me, to), device_id_type=MESH)

    def tile(k, h, c, t):
        return u_v[k, h, c, 16 * t:16 * t + 16].astype(F32).reshape(T, T)

    def accumulate(k, h):
        um = (um0, um1)[h]
        off = 2 * T * h
        pr = tile(k, h, 0, 0)
        pi = tile(k, h, 1, 0)
        um[0, off:off + T, 0:T] = jnp.where(row < col, pr, 0.0).astype(BF)
        um[1, off:off + T, 0:T] = jnp.where(row < col, pi, jnp.where(row == col, 0.5 * pi, 0.0)).astype(BF)
        um[0, off + T:off + 2 * T, T:] = jnp.where(row > col, pr, 0.0).astype(BF)
        um[1, off + T:off + 2 * T, T:] = jnp.where(row > col, pi, jnp.where(row == col, 0.5 * pr, 0.0)).astype(BF)
        for c in range(2):
            if h == 0:
                um[c, 0:T, T:] = tile(k, 0, c, 1).astype(BF)
            else:
                um[c, 0:T, 0:T] = tile(k, 0, c, 2).astype(BF)
                um[c, T:2 * T, 0:T] = tile(k, 0, c, 3).astype(BF)
                um[c, 0:T, T:] = tile(k, 1, c, 1).astype(BF)
                um[c, T:2 * T, T:] = tile(k, 1, c, 2).astype(BF)
                um[c, 2 * T:3 * T, T:] = tile(k, 1, c, 3).astype(BF)
        depth = 2 * T * (h + 1)

        @pl.loop(0, 2)
        def _(m):
            rows = pl.ds(pl.multiple_of(256 * m, 256), 256)
            rr = r_v[k, rows, 0:depth]
            ri = r_v[4 + k, rows, 0:depth]
            ur = um[0]
            ui = um[1]
            lr = (mm(rr, ur) - mm(ri, ui)).astype(BF)
            li = (mm(rr, ui) + mm(ri, ur)).astype(BF)
            tr = rt_v[k, off:off + 256, :]
            ti = rt_v[4 + k, off:off + 256, :]
            xr[rows, :] += mm(lr, tr) + mm(li, ti)
            xi[rows, :] += mm(li, tr) - mm(lr, ti)

    for h in range(CHUNKS):
        pltpu.make_async_copy(u_v.at[sp, h], u_v.at[sp, h], sgr.at[h]).wait()
        to_core = hop(sp, h, 0, sp_core)
        to_z = hop(sp, h, 1, sp_z)
        to_z.start()
        to_core.start()
        accumulate(sp, h)
        to_core.wait_recv()
        accumulate(sp_core, h)
        to_z.wait_recv()
        onward = hop(sp_z, h, 2, sp_core)
        onward.start()
        accumulate(sp_z, h)
        onward.wait_recv()
        accumulate(sp_zc, h)
        to_core.wait_send()
        to_z.wait_send()
        onward.wait_send()

    for h in range(CHUNKS):
        for t, (i, j) in enumerate(TILES[h]):
            pr = tile(sp, h, 0, t)
            pi = tile(sp, h, 1, t)
            prt = pr.T
            pit = pi.T
            a = slice(T * i, T * i + T)
            if i == j:
                b = slice(T * i + T, T * i + 2 * T)
                sig_ref[0, a, a] = jnp.where(row < col, pr, jnp.where(row > col, -prt, 0.0)).astype(BF)
                sig_ref[1, a, a] = jnp.where(row <= col, pi, pit).astype(BF)
                sig_ref[0, b, b] = jnp.where(row > col, pr, jnp.where(row < col, -prt, 0.0)).astype(BF)
                sig_ref[1, b, b] = jnp.where(row > col, pi, jnp.where(row < col, pit, pr)).astype(BF)
            else:
                b = slice(T * j, T * j + T)
                sig_ref[0, a, b] = pr.astype(BF)
                sig_ref[1, a, b] = pi.astype(BF)
                sig_ref[0, b, a] = (-prt).astype(BF)
                sig_ref[1, b, a] = pit.astype(BF)
    for i in range(4):
        for j in range(i, 4):
            a = slice(T * i, T * i + T)
            b = slice(T * j, T * j + T)
            dr = xr[a, b] - xr[b, a].T
            di = xi[a, b] + xi[b, a].T
            del_ref[0, a, b] = dr.astype(BF)
            del_ref[1, a, b] = di.astype(BF)
            if i != j:
                del_ref[0, b, a] = (-dr.T).astype(BF)
                del_ref[1, b, a] = di.T.astype(BF)

    for h in range(CHUNKS):
        pltpu.make_async_copy(send.at[h, 0:NE - 1], send.at[h, 0:NE - 1], gws.at[h]).wait()
        pltpu.make_async_copy(ssend.at[h, 0:NE - 1], ssend.at[h, 0:NE - 1], sgs.at[h]).wait()


def shards(g, w, r, idx):
    ft, bt, tw = tables()
    vmem = pl.BlockSpec(memory_space=pltpu.VMEM)
    hbm = pl.BlockSpec(memory_space=pl.ANY)
    out = jax.ShapeDtypeStruct((2, B, B), BF)
    dma = pltpu.SemaphoreType.DMA
    sig, delta = pl.pallas_call(
        body,
        name="gw",
        out_shape=(out, out),
        in_specs=[hbm, hbm, hbm, vmem, vmem, vmem, vmem],
        out_specs=(vmem, vmem),
        scratch_shapes=[
            pltpu.VMEM((2, B, B), BF),
            pltpu.VMEM((2, B, B), BF),
            pltpu.VMEM((8, B, B), BF),
            pltpu.VMEM((8, B, B), BF),
            pltpu.VMEM((CHUNKS, NE, 2, 2, 8, T), BF),
            pltpu.VMEM((CHUNKS, NE, 2, 2, 8, T), BF),
            pltpu.VMEM((CHUNKS, NE, 2, 8, T), BF),
            pltpu.VMEM((4, CHUNKS, 2, NE, 8, T), BF),
            pltpu.VMEM((2, 1024, T), F32),
            pltpu.VMEM((2, T, 10 * T), BF),
            pltpu.VMEM((2 * LEN, 10 * T), BF),
            pltpu.VMEM((2 * LEN, 10 * T), BF),
            pltpu.VMEM((2, 2 * LEN, T), BF),
            pltpu.VMEM((2, T, 2 * LEN), BF),
            pltpu.VMEM((2, 2 * T, 2 * T), BF),
            pltpu.VMEM((2, 4 * T, 2 * T), BF),
            pltpu.VMEM((B, B), F32),
            pltpu.VMEM((B, B), F32),
            dma((3,)),
            dma((CHUNKS,)),
            dma((CHUNKS,)),
            dma((CHUNKS,)),
            dma((CHUNKS,)),
            dma((CHUNKS, 3)),
            dma((CHUNKS, 3)),
        ],
        compiler_params=pltpu.CompilerParams(collective_id=0, has_side_effects=True,
                                             vmem_limit_bytes=48 * 1024 * 1024),
    )(g.reshape(2, B, B), w.reshape(2, B, B), r.reshape(8, B, B), idx.reshape(1, NE),
      jnp.asarray(ft), jnp.asarray(bt), jnp.asarray(tw))
    return sig.reshape(1, 2, 1, B, B), delta.reshape(1, 2, 1, B, B)


def solution(mesh):
    block = P("energy", None, "space", None, None)
    return jax.shard_map(
        shards,
        mesh=mesh,
        in_specs=(block, block, P("energy", None, "space", None, None, None), P()),
        out_specs=(block, block),
        check_vma=False,
    )
```

```python
import math

import jax
import jax.numpy as jnp
from jax import lax
from jax.experimental import pallas as pl
from jax.experimental.pallas import tpu as pltpu
from jax.sharding import PartitionSpec as P

MESH = pl.DeviceIdType.MESH
NE = 64
B = 512
T = 128
LEN = 96
TILES = (((0, 0), (0, 1)), ((2, 2), (0, 2)), ((1, 2), (2, 3)), ((0, 3), (1, 3)))
CHUNKS = len(TILES)
BF = jnp.bfloat16
F32 = jnp.float32


def mm(a, b):
    return jnp.dot(a, b, preferred_element_type=F32)


def body(g_hbm, w_hbm, r_hbm, idx_hbm, sig_ref, del_ref,
         g_v, w_v, idx_v, rc, rt, send, recv, ssend, u_v, scr, tmp,
         xb, ph, pw, fm, bm, ue, lcat, l3, x,
         lsem, gws, gwr, sgs, sgr, zs, zr, cs, cr):
    me = lax.axis_index("energy")
    sp = lax.axis_index("space")
    lo = sp // 2
    sp_core = lo * 2 + (sp + 1) % 2
    sp_z = (sp + 2) % 4
    sp_zc = (sp_core + 2) % 4
    order = (sp, sp_core, sp_z, sp_zc)
    zh = me // 4 % 4
    q_me = zh * 16 + me // 16 * 4 + me % 4
    za = zh
    zb = (zh + 3 + 2 * lo) % 4
    zc = (zh + 2) % 4
    zd = (zh + 1 + 2 * lo) % 4

    def ring(i):
        return lax.rem(me + i, NE)

    barrier = pltpu.get_barrier_semaphore()

    @pl.loop(1, NE)
    def _(i):
        pl.semaphore_signal(barrier, inc=1, device_id=(ring(i), sp), device_id_type=MESH)

    pl.semaphore_signal(barrier, inc=1, device_id=(me, sp_core), device_id_type=MESH)
    pl.semaphore_signal(barrier, inc=1, device_id=(me, sp_z), device_id_type=MESH)

    def tiles_of(h):
        for i, j in TILES[h]:
            for k in range(2 if i == j else 1):
                yield i + k, j + k

    def load(h, src, dst, i, j):
        at = (slice(None), slice(T * i, T * i + T), slice(T * j, T * j + T))
        return pltpu.make_async_copy(src.at[at], dst.at[at], lsem.at[h])

    for h in range(CHUNKS):
        for i, j in tiles_of(h):
            load(h, g_hbm, g_v, i, j).start()
            load(h, w_hbm, w_v, i, j).start()

    row = lax.broadcasted_iota(jnp.int32, (T, T), 0)
    col = lax.broadcasted_iota(jnp.int32, (T, T), 1)
    for h in range(CHUNKS):
        n_tiles = len(list(tiles_of(h)))
        all_of = g_v.at[:, 0:2 * T, 0:T * n_tiles]
        pltpu.make_async_copy(all_of, all_of, lsem.at[h]).wait()
        for t, (i, j) in enumerate(TILES[h]):
            for a, src in enumerate((g_v, w_v)):
                if i == j:
                    k = i + 1
                    d0r, d0i = (src[c, T * i:T * i + T, T * i:T * i + T].astype(F32) for c in range(2))
                    d1r, d1i = (src[c, T * k:T * k + T, T * k:T * k + T].astype(F32) for c in range(2))
                    both = (jnp.where(row < col, d0r, jnp.where(row > col, d1r, d1i)), jnp.where(row <= col, d0i, d1i))
                else:
                    both = [src[c, T * i:T * i + T, T * j:T * j + T].astype(F32) for c in range(2)]
                for c in range(2):
                    for n in range(4):
                        tmp[a, pl.ds(c * 4 + n, 32, stride=8), :] = both[c][32 * n:32 * n + 32]
                send[h, 32 * t:32 * t + 32, a] = tmp[a].reshape(32, 8, T).astype(BF)

        if h == 0:
            pl.semaphore_wait(barrier, NE + 1)

        @pl.loop(1, NE)
        def _(i):
            d = ring(i)
            q = lax.rem(lax.div(d, 4), 4) * 16 + lax.div(d, 16) * 4 + lax.rem(d, 4)
            pltpu.make_async_remote_copy(
                src_ref=send.at[h, q], dst_ref=recv.at[h, me], send_sem=gws.at[h], recv_sem=gwr.at[h],
                device_id=(d, sp), device_id_type=MESH).start()

        pltpu.make_async_copy(send.at[h, q_me], recv.at[h, me], gwr.at[h]).start()

    small = pltpu.make_async_copy(idx_hbm, idx_v, lsem.at[5])
    small.start()
    for n, k in enumerate(order):
        for c in range(2):
            for i in range(4):
                pltpu.make_async_copy(r_hbm.at[4 * c + k, :, T * i:T * i + T],
                                      rc.at[n, :, T * (2 * i + c):T * (2 * i + c) + T], lsem.at[4]).start()

    small.wait()

    def lines(shape, axis):
        return lax.broadcasted_iota(jnp.int32, shape, axis)

    twice = (lines((NE, T), 0) == lines((NE, T), 1) % NE).astype(F32).astype(BF)
    point = mm(jnp.broadcast_to(idx_v[...].astype(F32), (8, NE)).astype(BF), twice)[0:1, :]
    wide = (2 * LEN, T)
    out_c = (lines(wide, 0) >= LEN).astype(F32)
    freq = lines(wide, 0).astype(F32) - LEN * out_c
    in_c = (lines(wide, 1) >= NE).astype(F32)

    def wave(steps):
        turns = steps - LEN * jnp.floor((steps + 0.5) / LEN)
        return jnp.cos(turns * (2.0 * math.pi / LEN))

    def halves(m):
        high = m.astype(BF)
        return high, (m - high.astype(F32)).astype(BF)

    quarter = LEN // 4
    eye = (lines((2 * LEN, 2 * LEN), 0) == lines((2 * LEN, 2 * LEN), 1)).astype(F32).astype(BF)
    for a, m in enumerate(halves(wave(freq * point + quarter * (out_c - in_c)))):
        fm[a] = m
    for a, m in enumerate(halves(wave(freq * (point + NE // 2) + quarter * (1.0 - in_c + out_c)) * (NE**-0.5 / LEN))):
        bm[a] = lax.dot_general(m, eye, (((0,), (0,)), ((), ())), preferred_element_type=F32).astype(BF)

    pltpu.make_async_copy(rc, rc, lsem.at[4]).wait()

    @pl.loop(0, 4)
    def _(n):
        at = pl.multiple_of(n * 2 * T, 2 * T)
        for j in range(4):
            for i in range(4):
                r_t = rc[n, T * i:T * i + T, 2 * T * j:2 * T * j + T].astype(F32).T
                i_t = rc[n, T * i:T * i + T, 2 * T * j + T:2 * T * j + 2 * T].astype(F32).T
                rt[j, pl.ds(at, T), T * i:T * i + T] = r_t.astype(BF)
                rt[j, pl.ds(at, T), B + T * i:B + T * i + T] = (-i_t).astype(BF)
                rt[j, pl.ds(at + T, T), T * i:T * i + T] = i_t.astype(BF)
                rt[j, pl.ds(at + T, T), B + T * i:B + T * i + T] = r_t.astype(BF)

    def convolve(h):
        pltpu.make_async_copy(recv.at[h], recv.at[h], gwr.at[h]).wait()
        for a in range(2):
            scr[a] = recv[h, :, a].astype(F32).reshape(8 * NE, T)
        r = q_me % 32
        for a in range(2):
            diag = jnp.zeros((T, T), F32)
            for i in range(4):
                x_i = jnp.concatenate(
                    [scr[a, pl.ds(i, NE, stride=8), :], scr[a, pl.ds(4 + i, NE, stride=8), :]], axis=0)
                diag = jnp.where(col == 32 * i + r, x_i, diag)
                xb[a, :, T * i:T * i + T] = x_i.astype(BF)
            xb[a, :, 4 * T:5 * T] = jnp.where(row < NE, diag, 0.0).astype(BF)
            xb[a, :, 5 * T:] = jnp.where(row < NE, 0.0, diag).astype(BF)
        for n in range(3):
            cols = slice(256 * n, 256 * n + 256)
            gx = xb[0, :, cols]
            wx = xb[1, :, cols]
            gh = mm(fm[0], gx) + mm(fm[1], gx)
            wh = mm(fm[0], wx) + mm(fm[1], wx)
            pr = gh[:LEN] * wh[:LEN] - gh[LEN:] * wh[LEN:]
            pi = gh[:LEN] * wh[LEN:] + gh[LEN:] * wh[:LEN]
            prod = jnp.concatenate([pr, pi], axis=0)
            hi = prod.astype(BF)
            ph[:, cols] = hi
            pw[:, cols] = (prod - hi.astype(F32)).astype(BF)

        def back(cols):
            return mm(bm[0], ph[:, cols]) + mm(bm[1], ph[:, cols]) + mm(bm[0], pw[:, cols])

        y = back(slice(4 * T, 6 * T))
        fix = jnp.concatenate([-y[NE:, :T], y[NE:, T:]], axis=0)
        here = q_me < 32 if TILES[h][0][0] == TILES[h][0][1] else None
        for n in range(2):
            y = back(slice(256 * n, 256 * n + 256))
            for m in range(2):
                i = 2 * n + m
                z = y[:, T * m:T * m + T]
                if here is not None:
                    z = jnp.where((col == 32 * i + r) & here, fix, z)
                scr[0, pl.ds(i, NE, stride=8), :] = z[:NE]
                scr[0, pl.ds(4 + i, NE, stride=8), :] = z[NE:]
        ssend[h] = scr[0].reshape(NE, 8, T).astype(BF)

        @pl.loop(1, NE)
        def _(i):
            d = ring(i)
            far = lax.div(lax.rem(lax.rem(lax.div(d, 4), 4) - zh + 4 + lo, 4), 2)
            pltpu.make_async_remote_copy(
                src_ref=ssend.at[h, d], dst_ref=u_v.at[sp, h, q_me], send_sem=sgs.at[h], recv_sem=sgr.at[h],
                device_id=(d, lax.rem(sp + 2 * far, 4)), device_id_type=MESH).start()

        pltpu.make_async_copy(ssend.at[h, me], u_v.at[sp, h, q_me], sgr.at[h]).start()

    def part(k, h, z):
        return u_v.at[k, h, pl.ds(16 * z, 16)]

    def give(k, h, z, to, ss, rs):
        pltpu.make_async_remote_copy(
            src_ref=part(k, h, z), dst_ref=part(k, h, z), send_sem=ss, recv_sem=rs,
            device_id=(me, to), device_id_type=MESH).start()

    def whole(h, s):
        pltpu.make_async_copy(u_v.at[sp, h], u_v.at[sp, h], s).wait()

    first = ((sp, za), (sp, zb), (sp_z, zc), (sp_z, zb))
    second = ((sp, zc), (sp, zd), (sp_z, za), (sp_z, zd))

    def stage1(h):
        whole(h, sgr.at[h])
        for k, z in first:
            give(k, h, z, sp_z, zs.at[h], zr.at[h])
        for k, z in first:
            give(k, h, z, sp_core, cs.at[0, h], cr.at[0, h])

    def stage2(h):
        whole(h, zr.at[h])
        for k, z in second:
            give(k, h, z, sp_core, cs.at[1, h], cr.at[1, h])

    def stage3(h):
        whole(h, cr.at[0, h])
        whole(h, cr.at[1, h])

    def tile(k, h, t):
        tmp[t] = u_v[k, h, 32 * t:32 * t + 32].astype(F32).reshape(2 * T, T)
        return [jnp.concatenate([tmp[t, pl.ds(4 * c + n, 32, stride=8), :] for n in range(4)], axis=0) for c in range(2)]

    def put(n, at, p):
        ur, ui = p[0].astype(BF), p[1].astype(BF)
        ue[n, at:at + T, 0:T] = ur
        ue[n, at:at + T, T:2 * T] = ui
        ue[n, at + T:at + 2 * T, 0:T] = -ui
        ue[n, at + T:at + 2 * T, T:2 * T] = ur

    def upper(p):
        return (jnp.where(row < col, p[0], 0.0),
                jnp.where(row < col, p[1], jnp.where(row == col, 0.5 * p[1], 0.0)))

    def lower(p):
        return (jnp.where(row > col, p[0], 0.0),
                jnp.where(row > col, p[1], jnp.where(row == col, 0.5 * p[0], 0.0)))

    def left(n, i, depth):
        return mm(rc[n, :, 2 * T * i:2 * T * (i + depth)], ue[n, 2 * T * i:2 * T * (i + depth), :])

    def product(h):
        for n, k in enumerate(order):
            at = 2 * T * n
            p = tile(k, h, 0)
            s = tile(k, h, 1)
            if h == 0:
                put(n, 0, upper(p))
                lcat[:, at:at + 2 * T] = left(n, 0, 1).astype(BF)
                put(n, 0, s)
                put(n, 2 * T, lower(p))
                lcat[:, 1024 + at:1024 + at + 2 * T] = left(n, 0, 2).astype(BF)
            elif h == 2:
                d = tile(k, 1, 0)
                put(n, 0, tile(k, 1, 1))
                put(n, 2 * T, p)
                put(n, 4 * T, upper(d))
                lcat[:, at:at + 2 * T] = left(n, 0, 3).astype(BF)
                put(n, 4 * T, s)
                put(n, 6 * T, lower(d))
                l3[n] = left(n, 2, 2)
            else:
                put(n, 0, p)
                put(n, 2 * T, s)
                lcat[:, at:at + 2 * T] = (l3[n] + left(n, 0, 2)).astype(BF)

        for m in range(4):
            cols = slice(256 * m, 256 * m + 256)
            if h == 0:
                x[:, cols] = mm(lcat[:, :1024], rt[0, :, cols])
                x[:, cols] += mm(lcat[:, 1024:], rt[1, :, cols])
            else:
                x[:, cols] += mm(lcat[:, :1024], rt[2 if h == 2 else 3, :, cols])

    def sigma_out(h):
        for t, (i, j) in enumerate(TILES[h]):
            pr, pi = tile(sp, h, t)
            prt = pr.T
            pit = pi.T
            a = slice(T * i, T * i + T)
            if i == j:
                b = slice(T * i + T, T * i + 2 * T)
                sig_ref[0, a, a] = jnp.where(row < col, pr, jnp.where(row > col, -prt, 0.0)).astype(BF)
                sig_ref[1, a, a] = jnp.where(row <= col, pi, pit).astype(BF)
                sig_ref[0, b, b] = jnp.where(row > col, pr, jnp.where(row < col, -prt, 0.0)).astype(BF)
                sig_ref[1, b, b] = jnp.where(row > col, pi, jnp.where(row < col, pit, pr)).astype(BF)
            else:
                b = slice(T * j, T * j + T)
                sig_ref[0, a, b] = pr.astype(BF)
                sig_ref[1, a, b] = pi.astype(BF)
                sig_ref[0, b, a] = (-prt).astype(BF)
                sig_ref[1, b, a] = pit.astype(BF)

    for h in range(CHUNKS):
        convolve(h)
    stage1(0)
    stage1(1)
    stage2(0)
    stage1(2)
    stage2(1)
    stage3(0)
    product(0)
    stage1(3)
    stage2(2)
    stage3(1)
    stage3(2)
    sigma_out(0)
    sigma_out(1)
    product(2)
    stage2(3)
    sigma_out(2)
    sigma_out(3)
    stage3(3)
    product(3)

    for i in range(4):
        for j in range(i, 4):
            a = slice(T * i, T * i + T)
            b = slice(T * j, T * j + T)
            a2 = slice(B + T * i, B + T * i + T)
            b2 = slice(B + T * j, B + T * j + T)
            dr = x[a, b] - x[b, a].T
            di = x[a, b2] + x[b, a2].T
            del_ref[0, a, b] = dr.astype(BF)
            del_ref[1, a, b] = di.astype(BF)
            if i != j:
                del_ref[0, b, a] = (-dr.T).astype(BF)
                del_ref[1, b, a] = di.T.astype(BF)

    for h in range(CHUNKS):
        pltpu.make_async_copy(send.at[h, 0:NE - 1], send.at[h, 0:NE - 1], gws.at[h]).wait()
        pltpu.make_async_copy(ssend.at[h, 0:NE - 1], ssend.at[h, 0:NE - 1], sgs.at[h]).wait()
        whole(h, zs.at[h])
        whole(h, cs.at[0, h])
        whole(h, cs.at[1, h])


def shards(g, w, r, idx):
    vmem = pl.BlockSpec(memory_space=pltpu.VMEM)
    hbm = pl.BlockSpec(memory_space=pltpu.HBM)
    out = jax.ShapeDtypeStruct((2, B, B), BF)
    dma = pltpu.SemaphoreType.DMA
    sig, delta = pl.pallas_call(
        body,
        name="gw",
        out_shape=(out, out),
        in_specs=[hbm] * 4,
        out_specs=(vmem, vmem),
        scratch_shapes=[
            pltpu.VMEM((2, B, B), BF),
            pltpu.VMEM((2, B, B), BF),
            pltpu.VMEM((1, NE), jnp.int32),
            pltpu.VMEM((4, B, 2 * B), BF),
            pltpu.VMEM((4, 2 * B, 2 * B), BF),
            pltpu.VMEM((CHUNKS, NE, 2, 8, T), BF),
            pltpu.VMEM((CHUNKS, NE, 2, 8, T), BF),
            pltpu.VMEM((CHUNKS, NE, 8, T), BF),
            pltpu.VMEM((4, CHUNKS, NE, 8, T), BF),
            pltpu.VMEM((2, 8 * NE, T), F32),
            pltpu.VMEM((2, 2 * T, T), F32),
            pltpu.VMEM((2, T, 6 * T), BF),
            pltpu.VMEM((2 * LEN, 6 * T), BF),
            pltpu.VMEM((2 * LEN, 6 * T), BF),
            pltpu.VMEM((2, 2 * LEN, T), BF),
            pltpu.VMEM((2, T, 2 * LEN), BF),
            pltpu.VMEM((4, 8 * T, 2 * T), BF),
            pltpu.VMEM((B, 4 * B), BF),
            pltpu.VMEM((4, B, 2 * T), F32),
            pltpu.VMEM((B, 2 * B), F32),
            dma((6,)),
            dma((CHUNKS,)),
            dma((CHUNKS,)),
            dma((CHUNKS,)),
            dma((CHUNKS,)),
            dma((CHUNKS,)),
            dma((CHUNKS,)),
            dma((2, CHUNKS)),
            dma((2, CHUNKS)),
        ],
        compiler_params=pltpu.CompilerParams(collective_id=0, has_side_effects=True,
                                             vmem_limit_bytes=51 * 1024 * 1024),
    )(g.reshape(2, B, B), w.reshape(2, B, B), r.reshape(8, B, B), idx.reshape(1, NE))
    return sig.reshape(1, 2, 1, B, B), delta.reshape(1, 2, 1, B, B)


def solution(mesh):
    block = P("energy", None, "space", None, None)
    return jax.shard_map(
        shards,
        mesh=mesh,
        in_specs=(block, block, P("energy", None, "space", None, None, None), P()),
        out_specs=(block, block),
        check_vma=False,
    )
```

```python
import math

import jax
import jax.numpy as jnp
from jax import lax
from jax.experimental import pallas as pl
from jax.experimental.pallas import tpu as pltpu
from jax.sharding import PartitionSpec as P

MESH = pl.DeviceIdType.MESH
NE = 64
B = 512
T = 128
LEN = 96
TILES = (((0, 0), (0, 1)), ((2, 2), (0, 2)), ((1, 2), (2, 3)), ((0, 3), (1, 3)))
CHUNKS = len(TILES)
BF = jnp.bfloat16
F32 = jnp.float32


def mm(a, b):
    return jnp.dot(a, b, preferred_element_type=F32)


def body(g_hbm, w_hbm, r_hbm, idx_hbm, sig_ref, del_ref,
         g_v, w_v, idx_v, rc, rt, send, recv, ssend, u_v, scr, tmp,
         xb, ph, pw, fm, bm, ue, lcat, l3, x,
         lsem, gws, gwr, sgs, sgr, zs, zr, cs, cr):
    me = lax.axis_index("energy")
    sp = lax.axis_index("space")
    lo = sp // 2
    sp_core = lo * 2 + (sp + 1) % 2
    sp_z = (sp + 2) % 4
    sp_zc = (sp_core + 2) % 4
    order = (sp, sp_z, sp_core, sp_zc)
    zh = me // 4 % 4
    q_me = zh * 16 + me // 16 * 4 + me % 4
    za = zh
    zb = (zh + 3 + 2 * lo) % 4
    zc = (zh + 2) % 4
    zd = (zh + 1 + 2 * lo) % 4

    def ring(i):
        return lax.rem(me + i, NE)

    barrier = pltpu.get_barrier_semaphore()

    @pl.loop(1, NE)
    def _(i):
        pl.semaphore_signal(barrier, inc=1, device_id=(ring(i), sp), device_id_type=MESH)

    pl.semaphore_signal(barrier, inc=1, device_id=(me, sp_core), device_id_type=MESH)
    pl.semaphore_signal(barrier, inc=1, device_id=(me, sp_z), device_id_type=MESH)

    def tiles_of(h):
        for i, j in TILES[h]:
            for k in range(2 if i == j else 1):
                yield i + k, j + k

    def load(h, src, dst, i, j):
        at = (slice(None), slice(T * i, T * i + T), slice(T * j, T * j + T))
        return pltpu.make_async_copy(src.at[at], dst.at[at], lsem.at[h])

    for h in range(CHUNKS):
        for i, j in tiles_of(h):
            load(h, g_hbm, g_v, i, j).start()
            load(h, w_hbm, w_v, i, j).start()

    row = lax.broadcasted_iota(jnp.int32, (T, T), 0)
    col = lax.broadcasted_iota(jnp.int32, (T, T), 1)
    for h in range(CHUNKS):
        n_tiles = len(list(tiles_of(h)))
        all_of = g_v.at[:, 0:2 * T, 0:T * n_tiles]
        pltpu.make_async_copy(all_of, all_of, lsem.at[h]).wait()
        for t, (i, j) in enumerate(TILES[h]):
            for a, src in enumerate((g_v, w_v)):
                if i == j:
                    k = i + 1
                    d0r, d0i = (src[c, T * i:T * i + T, T * i:T * i + T].astype(F32) for c in range(2))
                    d1r, d1i = (src[c, T * k:T * k + T, T * k:T * k + T].astype(F32) for c in range(2))
                    both = (jnp.where(row < col, d0r, jnp.where(row > col, d1r, d1i)), jnp.where(row <= col, d0i, d1i))
                else:
                    both = [src[c, T * i:T * i + T, T * j:T * j + T].astype(F32) for c in range(2)]
                for c in range(2):
                    for n in range(4):
                        tmp[a, pl.ds(c * 4 + n, 32, stride=8), :] = both[c][32 * n:32 * n + 32]
                send[h, 32 * t:32 * t + 32, a] = tmp[a].reshape(32, 8, T).astype(BF)

        if h == 0:
            pl.semaphore_wait(barrier, NE + 1)

        @pl.loop(1, NE)
        def _(i):
            d = ring(i)
            q = lax.rem(lax.div(d, 4), 4) * 16 + lax.div(d, 16) * 4 + lax.rem(d, 4)
            pltpu.make_async_remote_copy(
                src_ref=send.at[h, q], dst_ref=recv.at[h, me], send_sem=gws.at[h], recv_sem=gwr.at[h],
                device_id=(d, sp), device_id_type=MESH).start()

        pltpu.make_async_copy(send.at[h, q_me], recv.at[h, me], gwr.at[h]).start()

    small = pltpu.make_async_copy(idx_hbm, idx_v, lsem.at[5])
    small.start()
    for n, k in enumerate(order):
        for c in range(2):
            for i in range(4):
                pltpu.make_async_copy(r_hbm.at[4 * c + k, :, T * i:T * i + T],
                                      rc.at[n, :, T * (2 * i + c):T * (2 * i + c) + T], lsem.at[4]).start()

    small.wait()

    def lines(shape, axis):
        return lax.broadcasted_iota(jnp.int32, shape, axis)

    twice = (lines((NE, T), 0) == lines((NE, T), 1) % NE).astype(F32).astype(BF)
    point = mm(jnp.broadcast_to(idx_v[...].astype(F32), (8, NE)).astype(BF), twice)[0:1, :]
    wide = (2 * LEN, T)
    out_c = (lines(wide, 0) >= LEN).astype(F32)
    freq = lines(wide, 0).astype(F32) - LEN * out_c
    in_c = (lines(wide, 1) >= NE).astype(F32)

    def wave(steps):
        turns = steps - LEN * jnp.floor((steps + 0.5) / LEN)
        return jnp.cos(turns * (2.0 * math.pi / LEN))

    def halves(m):
        high = m.astype(BF)
        return high, (m - high.astype(F32)).astype(BF)

    quarter = LEN // 4
    eye = (lines((2 * LEN, 2 * LEN), 0) == lines((2 * LEN, 2 * LEN), 1)).astype(F32).astype(BF)
    for a, m in enumerate(halves(wave(freq * point + quarter * (out_c - in_c)))):
        fm[a] = m
    for a, m in enumerate(halves(wave(freq * (point + NE // 2) + quarter * (1.0 - in_c + out_c)) * (NE**-0.5 / LEN))):
        bm[a] = lax.dot_general(m, eye, (((0,), (0,)), ((), ())), preferred_element_type=F32).astype(BF)

    pltpu.make_async_copy(rc, rc, lsem.at[4]).wait()

    @pl.loop(0, 4)
    def _(n):
        at = pl.multiple_of(n * 2 * T, 2 * T)
        for j in range(4):
            for i in range(4):
                r_t = rc[n, T * i:T * i + T, 2 * T * j:2 * T * j + T].astype(F32).T
                i_t = rc[n, T * i:T * i + T, 2 * T * j + T:2 * T * j + 2 * T].astype(F32).T
                rt[j, pl.ds(at, T), T * i:T * i + T] = r_t.astype(BF)
                rt[j, pl.ds(at, T), B + T * i:B + T * i + T] = (-i_t).astype(BF)
                rt[j, pl.ds(at + T, T), T * i:T * i + T] = i_t.astype(BF)
                rt[j, pl.ds(at + T, T), B + T * i:B + T * i + T] = r_t.astype(BF)

    def convolve(h):
        pltpu.make_async_copy(recv.at[h], recv.at[h], gwr.at[h]).wait()
        for a in range(2):
            scr[a] = recv[h, :, a].astype(F32).reshape(8 * NE, T)
        r = q_me % 32
        for a in range(2):
            diag = jnp.zeros((T, T), F32)
            for i in range(4):
                x_i = jnp.concatenate(
                    [scr[a, pl.ds(i, NE, stride=8), :], scr[a, pl.ds(4 + i, NE, stride=8), :]], axis=0)
                diag = jnp.where(col == 32 * i + r, x_i, diag)
                xb[a, :, T * i:T * i + T] = x_i.astype(BF)
            xb[a, :, 4 * T:5 * T] = jnp.where(row < NE, diag, 0.0).astype(BF)
            xb[a, :, 5 * T:] = jnp.where(row < NE, 0.0, diag).astype(BF)
        for n in range(3):
            cols = slice(256 * n, 256 * n + 256)
            gx = xb[0, :, cols]
            wx = xb[1, :, cols]
            gh = mm(fm[0], gx) + mm(fm[1], gx)
            wh = mm(fm[0], wx) + mm(fm[1], wx)
            pr = gh[:LEN] * wh[:LEN] - gh[LEN:] * wh[LEN:]
            pi = gh[:LEN] * wh[LEN:] + gh[LEN:] * wh[:LEN]
            prod = jnp.concatenate([pr, pi], axis=0)
            hi = prod.astype(BF)
            ph[:, cols] = hi
            pw[:, cols] = (prod - hi.astype(F32)).astype(BF)

        def back(cols):
            return mm(bm[0], ph[:, cols]) + mm(bm[1], ph[:, cols]) + mm(bm[0], pw[:, cols])

        y = back(slice(4 * T, 6 * T))
        fix = jnp.concatenate([-y[NE:, :T], y[NE:, T:]], axis=0)
        here = q_me < 32 if TILES[h][0][0] == TILES[h][0][1] else None
        for n in range(2):
            y = back(slice(256 * n, 256 * n + 256))
            for m in range(2):
                i = 2 * n + m
                z = y[:, T * m:T * m + T]
                if here is not None:
                    z = jnp.where((col == 32 * i + r) & here, fix, z)
                scr[0, pl.ds(i, NE, stride=8), :] = z[:NE]
                scr[0, pl.ds(4 + i, NE, stride=8), :] = z[NE:]
        ssend[h] = scr[0].reshape(NE, 8, T).astype(BF)

        @pl.loop(1, NE)
        def _(i):
            d = ring(i)
            away = lax.rem((1 - 2 * lo) * (lax.rem(lax.div(d, 4), 4) - zh) + 4, 4)
            far = lax.div(away, 2)
            kind = away + far * (5 - 2 * away)
            pltpu.make_async_remote_copy(
                src_ref=ssend.at[h, d], dst_ref=u_v.at[sp, h, q_me], send_sem=sgs.at[h], recv_sem=sgr.at[h, kind],
                device_id=(d, lax.rem(sp + 2 * far, 4)), device_id_type=MESH).start()

        pltpu.make_async_copy(ssend.at[h, me], u_v.at[sp, h, q_me], sgr.at[h, 0]).start()

    def part(k, h, z):
        return u_v.at[k, h, pl.ds(16 * z, 16)]

    def give(k, h, z, to, ss, rs):
        pltpu.make_async_remote_copy(
            src_ref=part(k, h, z), dst_ref=part(k, h, z), send_sem=ss, recv_sem=rs,
            device_id=(me, to), device_id_type=MESH).start()

    def whole(h, s):
        pltpu.make_async_copy(u_v.at[sp, h], u_v.at[sp, h], s).wait()

    first = ((sp, za), (sp, zb), (sp_z, zb), (sp_z, zc))
    second = ((sp_z, za), (sp_z, zd), (sp, zd), (sp, zc))

    def stage1(h, kinds=range(4)):
        for n in kinds:
            k, z = first[n]
            pltpu.make_async_copy(part(k, h, z), part(k, h, z), sgr.at[h, n]).wait()
            give(k, h, z, sp_z, zs.at[h], zr.at[h, n])
            give(k, h, z, sp_core, cs.at[0, h], cr.at[0, h])

    def stage2(h, kinds=range(4)):
        for n in kinds:
            k, z = second[n]
            pltpu.make_async_copy(part(k, h, z), part(k, h, z), zr.at[h, n]).wait()
            give(k, h, z, sp_core, cs.at[1, h], cr.at[1, h])

    def stage3(h):
        whole(h, cr.at[0, h])
        whole(h, cr.at[1, h])

    def tile(k, h, t):
        tmp[t] = u_v[k, h, 32 * t:32 * t + 32].astype(F32).reshape(2 * T, T)
        return [jnp.concatenate([tmp[t, pl.ds(4 * c + n, 32, stride=8), :] for n in range(4)], axis=0) for c in range(2)]

    def put(n, at, p):
        ur, ui = p[0].astype(BF), p[1].astype(BF)
        ue[n, at:at + T, 0:T] = ur
        ue[n, at:at + T, T:2 * T] = ui
        ue[n, at + T:at + 2 * T, 0:T] = -ui
        ue[n, at + T:at + 2 * T, T:2 * T] = ur

    def upper(p):
        return (jnp.where(row < col, p[0], 0.0),
                jnp.where(row < col, p[1], jnp.where(row == col, 0.5 * p[1], 0.0)))

    def lower(p):
        return (jnp.where(row > col, p[0], 0.0),
                jnp.where(row > col, p[1], jnp.where(row == col, 0.5 * p[0], 0.0)))

    def left(n, i, depth):
        return mm(rc[n, :, 2 * T * i:2 * T * (i + depth)], ue[n, 2 * T * i:2 * T * (i + depth), :])

    def place(n):
        return slice(2 * T * n, 2 * T * n + 2 * T)

    def rows01(n):
        put(n, 0, upper(tile(order[n], 0, 0)))
        lcat[:, place(n)] = left(n, 0, 1).astype(BF)
        put(n, 0, tile(order[n], 0, 1))
        put(n, 2 * T, lower(tile(order[n], 0, 0)))
        lcat[:, place(4 + n)] = left(n, 0, 2).astype(BF)

    def rows2(n):
        put(n, 0, tile(order[n], 1, 1))
        put(n, 2 * T, tile(order[n], 2, 0))
        put(n, 4 * T, upper(tile(order[n], 1, 0)))
        lcat[:, place(n)] = left(n, 0, 3).astype(BF)
        put(n, 4 * T, tile(order[n], 2, 1))
        put(n, 6 * T, lower(tile(order[n], 1, 0)))
        l3[n] = left(n, 2, 2)

    def rows3(n):
        put(n, 0, tile(order[n], 3, 0))
        put(n, 2 * T, tile(order[n], 3, 1))
        lcat[:, place(4 + n)] = (l3[n] + left(n, 0, 2)).astype(BF)

    def total(j, at, depth):
        k = slice(2 * T * at, 2 * T * (at + depth))
        c = slice(1024 * (j % 2) + 2 * T * at, 1024 * (j % 2) + 2 * T * (at + depth))
        for m in range(4):
            cols = slice(256 * m, 256 * m + 256)
            y = mm(lcat[:, c], rt[j, k, cols])
            x[:, cols] = y if j == 0 else x[:, cols] + y

    def sigma_out(h):
        for t, (i, j) in enumerate(TILES[h]):
            pr, pi = tile(sp, h, t)
            prt = pr.T
            pit = pi.T
            a = slice(T * i, T * i + T)
            if i == j:
                b = slice(T * i + T, T * i + 2 * T)
                sig_ref[0, a, a] = jnp.where(row < col, pr, jnp.where(row > col, -prt, 0.0)).astype(BF)
                sig_ref[1, a, a] = jnp.where(row <= col, pi, pit).astype(BF)
                sig_ref[0, b, b] = jnp.where(row > col, pr, jnp.where(row < col, -prt, 0.0)).astype(BF)
                sig_ref[1, b, b] = jnp.where(row > col, pi, jnp.where(row < col, pit, pr)).astype(BF)
            else:
                b = slice(T * j, T * j + T)
                sig_ref[0, a, b] = pr.astype(BF)
                sig_ref[1, a, b] = pi.astype(BF)
                sig_ref[0, b, a] = (-prt).astype(BF)
                sig_ref[1, b, a] = pit.astype(BF)

    convolve(0)
    convolve(1)
    stage1(0, (0,))
    convolve(2)
    stage1(1, (0,))
    convolve(3)
    stage1(2, (0,))
    stage1(0, (1, 2, 3))
    stage1(1, (1, 2, 3))
    stage2(0)
    rows01(0)
    rows01(1)
    stage1(3, (0,))
    stage1(2, (1, 2, 3))
    stage2(1)
    sigma_out(0)
    sigma_out(1)
    stage3(0)
    rows01(2)
    rows01(3)
    total(0, 0, 4)
    stage1(3, (1, 2, 3))
    stage2(2)
    total(1, 0, 4)
    rows2(0)
    rows2(1)
    stage2(3)
    stage3(1)
    stage3(2)
    rows2(2)
    rows2(3)
    total(2, 0, 4)
    rows3(0)
    rows3(1)
    total(3, 0, 2)
    sigma_out(2)
    sigma_out(3)
    stage3(3)
    rows3(2)
    rows3(3)
    total(3, 2, 2)

    for i in range(4):
        for j in range(i, 4):
            a = slice(T * i, T * i + T)
            b = slice(T * j, T * j + T)
            a2 = slice(B + T * i, B + T * i + T)
            b2 = slice(B + T * j, B + T * j + T)
            dr = x[a, b] - x[b, a].T
            di = x[a, b2] + x[b, a2].T
            del_ref[0, a, b] = dr.astype(BF)
            del_ref[1, a, b] = di.astype(BF)
            if i != j:
                del_ref[0, b, a] = (-dr.T).astype(BF)
                del_ref[1, b, a] = di.T.astype(BF)

    for h in range(CHUNKS):
        pltpu.make_async_copy(send.at[h, 0:NE - 1], send.at[h, 0:NE - 1], gws.at[h]).wait()
        pltpu.make_async_copy(ssend.at[h, 0:NE - 1], ssend.at[h, 0:NE - 1], sgs.at[h]).wait()
        whole(h, zs.at[h])
        whole(h, cs.at[0, h])
        whole(h, cs.at[1, h])


def shards(g, w, r, idx):
    vmem = pl.BlockSpec(memory_space=pltpu.VMEM)
    hbm = pl.BlockSpec(memory_space=pltpu.HBM)
    out = jax.ShapeDtypeStruct((2, B, B), BF)
    dma = pltpu.SemaphoreType.DMA
    sig, delta = pl.pallas_call(
        body,
        name="gw",
        out_shape=(out, out),
        in_specs=[hbm] * 4,
        out_specs=(vmem, vmem),
        scratch_shapes=[
            pltpu.VMEM((2, B, B), BF),
            pltpu.VMEM((2, B, B), BF),
            pltpu.VMEM((1, NE), jnp.int32),
            pltpu.VMEM((4, B, 2 * B), BF),
            pltpu.VMEM((4, 2 * B, 2 * B), BF),
            pltpu.VMEM((CHUNKS, NE, 2, 8, T), BF),
            pltpu.VMEM((CHUNKS, NE, 2, 8, T), BF),
            pltpu.VMEM((CHUNKS, NE, 8, T), BF),
            pltpu.VMEM((4, CHUNKS, NE, 8, T), BF),
            pltpu.VMEM((2, 8 * NE, T), F32),
            pltpu.VMEM((2, 2 * T, T), F32),
            pltpu.VMEM((2, T, 6 * T), BF),
            pltpu.VMEM((2 * LEN, 6 * T), BF),
            pltpu.VMEM((2 * LEN, 6 * T), BF),
            pltpu.VMEM((2, 2 * LEN, T), BF),
            pltpu.VMEM((2, T, 2 * LEN), BF),
            pltpu.VMEM((4, 8 * T, 2 * T), BF),
            pltpu.VMEM((B, 4 * B), BF),
            pltpu.VMEM((4, B, 2 * T), F32),
            pltpu.VMEM((B, 2 * B), F32),
            dma((6,)),
            dma((CHUNKS,)),
            dma((CHUNKS,)),
            dma((CHUNKS,)),
            dma((CHUNKS, 4)),
            dma((CHUNKS,)),
            dma((CHUNKS, 4)),
            dma((2, CHUNKS)),
            dma((2, CHUNKS)),
        ],
        compiler_params=pltpu.CompilerParams(collective_id=0, has_side_effects=True,
                                             vmem_limit_bytes=51 * 1024 * 1024),
    )(g.reshape(2, B, B), w.reshape(2, B, B), r.reshape(8, B, B), idx.reshape(1, NE))
    return sig.reshape(1, 2, 1, B, B), delta.reshape(1, 2, 1, B, B)


def solution(mesh):
    block = P("energy", None, "space", None, None)
    return jax.shard_map(
        shards,
        mesh=mesh,
        in_specs=(block, block, P("energy", None, "space", None, None, None), P()),
        out_specs=(block, block),
        check_vma=False,
    )
```

```python
import math

import jax
import jax.numpy as jnp
from jax import lax
from jax.experimental import pallas as pl
from jax.experimental.pallas import tpu as pltpu
from jax.sharding import PartitionSpec as P

MESH = pl.DeviceIdType.MESH
NE = 64
B = 512
T = 128
LEN = 96
TILES = (((0, 0), (0, 1)), ((2, 2), (0, 2)), ((1, 2), (2, 3)), ((0, 3), (1, 3)))
CHUNKS = len(TILES)
BF = jnp.bfloat16
F32 = jnp.float32


def mm(a, b):
    return jnp.dot(a, b, preferred_element_type=F32)


def body(g_hbm, w_hbm, r_hbm, idx_hbm, sig_ref, xr, xi,
         g_v, w_v, idx_v, rc, rt, send, recv, ssend, u_v, scr, tmp,
         xb, ph, pw, fm, bm, ue, lcat, l3,
         lsem, gws, gwr, sgs, sgr, zs, zr, cs, cr):
    me = lax.axis_index("energy")
    sp = lax.axis_index("space")
    lo = sp // 2
    sp_core = lo * 2 + (sp + 1) % 2
    sp_z = (sp + 2) % 4
    sp_zc = (sp_core + 2) % 4
    order = (sp, sp_z, sp_core, sp_zc)
    zh = me // 4 % 4
    q_me = zh * 16 + me // 16 * 4 + me % 4
    za = zh
    zb = (zh + 3 + 2 * lo) % 4
    zc = (zh + 2) % 4
    zd = (zh + 1 + 2 * lo) % 4

    def ring(i):
        return lax.rem(me + i, NE)

    barrier = pltpu.get_barrier_semaphore()

    @pl.loop(1, NE)
    def _(i):
        pl.semaphore_signal(barrier, inc=1, device_id=(ring(i), sp), device_id_type=MESH)

    pl.semaphore_signal(barrier, inc=1, device_id=(me, sp_core), device_id_type=MESH)
    pl.semaphore_signal(barrier, inc=1, device_id=(me, sp_z), device_id_type=MESH)

    def tiles_of(h):
        for i, j in TILES[h]:
            for k in range(2 if i == j else 1):
                yield i + k, j + k

    def load(h, src, dst, i, j):
        at = (slice(None), slice(T * i, T * i + T), slice(T * j, T * j + T))
        return pltpu.make_async_copy(src.at[at], dst.at[at], lsem.at[h])

    for h in range(CHUNKS):
        for i, j in tiles_of(h):
            load(h, g_hbm, g_v, i, j).start()
            load(h, w_hbm, w_v, i, j).start()

    row = lax.broadcasted_iota(jnp.int32, (T, T), 0)
    col = lax.broadcasted_iota(jnp.int32, (T, T), 1)
    for h in range(CHUNKS):
        n_tiles = len(list(tiles_of(h)))
        all_of = g_v.at[:, 0:2 * T, 0:T * n_tiles]
        pltpu.make_async_copy(all_of, all_of, lsem.at[h]).wait()
        for t, (i, j) in enumerate(TILES[h]):
            for a, src in enumerate((g_v, w_v)):
                if i == j:
                    k = i + 1
                    d0r, d0i = (src[c, T * i:T * i + T, T * i:T * i + T].astype(F32) for c in range(2))
                    d1r, d1i = (src[c, T * k:T * k + T, T * k:T * k + T].astype(F32) for c in range(2))
                    both = (jnp.where(row < col, d0r, jnp.where(row > col, d1r, d1i)), jnp.where(row <= col, d0i, d1i))
                else:
                    both = [src[c, T * i:T * i + T, T * j:T * j + T].astype(F32) for c in range(2)]
                for c in range(2):
                    for n in range(4):
                        tmp[a, pl.ds(c * 4 + n, 32, stride=8), :] = both[c][32 * n:32 * n + 32]
                send[h, 32 * t:32 * t + 32, a] = tmp[a].reshape(32, 8, T).astype(BF)

        if h == 0:
            pl.semaphore_wait(barrier, NE + 1)

        @pl.loop(1, NE)
        def _(i):
            d = ring(i)
            q = lax.rem(lax.div(d, 4), 4) * 16 + lax.div(d, 16) * 4 + lax.rem(d, 4)
            pltpu.make_async_remote_copy(
                src_ref=send.at[h, q], dst_ref=recv.at[h, me], send_sem=gws.at[h], recv_sem=gwr.at[h],
                device_id=(d, sp), device_id_type=MESH).start()

        pltpu.make_async_copy(send.at[h, q_me], recv.at[h, me], gwr.at[h]).start()

    small = pltpu.make_async_copy(idx_hbm, idx_v, lsem.at[5])
    small.start()
    for n, k in enumerate(order):
        for c in range(2):
            for i in range(4):
                pltpu.make_async_copy(r_hbm.at[4 * c + k, :, T * i:T * i + T],
                                      rc.at[n, :, T * (2 * i + c):T * (2 * i + c) + T], lsem.at[4]).start()

    small.wait()

    def lines(shape, axis):
        return lax.broadcasted_iota(jnp.int32, shape, axis)

    twice = (lines((NE, T), 0) == lines((NE, T), 1) % NE).astype(F32).astype(BF)
    point = mm(jnp.broadcast_to(idx_v[...].astype(F32), (8, NE)).astype(BF), twice)[0:1, :]
    wide = (2 * LEN, T)
    out_c = (lines(wide, 0) >= LEN).astype(F32)
    freq = lines(wide, 0).astype(F32) - LEN * out_c
    in_c = (lines(wide, 1) >= NE).astype(F32)

    def wave(steps):
        turns = steps - LEN * jnp.floor((steps + 0.5) / LEN)
        return jnp.cos(turns * (2.0 * math.pi / LEN))

    def halves(m):
        high = m.astype(BF)
        return high, (m - high.astype(F32)).astype(BF)

    quarter = LEN // 4
    eye = (lines((2 * LEN, 2 * LEN), 0) == lines((2 * LEN, 2 * LEN), 1)).astype(F32).astype(BF)
    for a, m in enumerate(halves(wave(freq * point + quarter * (out_c - in_c)))):
        fm[a] = m
    for a, m in enumerate(halves(wave(freq * (point + NE // 2) + quarter * (1.0 - in_c + out_c)) * (NE**-0.5 / LEN))):
        bm[a] = lax.dot_general(m, eye, (((0,), (0,)), ((), ())), preferred_element_type=F32).astype(BF)

    pltpu.make_async_copy(rc, rc, lsem.at[4]).wait()

    @pl.loop(0, 4)
    def _(n):
        at = pl.multiple_of(n * 2 * T, 2 * T)
        for j in range(4):
            for i in range(4):
                r_t = rc[n, T * i:T * i + T, 2 * T * j:2 * T * j + T].astype(F32).T
                i_t = rc[n, T * i:T * i + T, 2 * T * j + T:2 * T * j + 2 * T].astype(F32).T
                rt[j, pl.ds(at, T), T * i:T * i + T] = r_t.astype(BF)
                rt[j, pl.ds(at, T), B + T * i:B + T * i + T] = (-i_t).astype(BF)
                rt[j, pl.ds(at + T, T), T * i:T * i + T] = i_t.astype(BF)
                rt[j, pl.ds(at + T, T), B + T * i:B + T * i + T] = r_t.astype(BF)

    def convolve(h):
        pltpu.make_async_copy(recv.at[h], recv.at[h], gwr.at[h]).wait()
        for a in range(2):
            scr[a] = recv[h, :, a].astype(F32).reshape(8 * NE, T)
        r = q_me % 32
        for a in range(2):
            diag = jnp.zeros((T, T), F32)
            for i in range(4):
                x_i = jnp.concatenate(
                    [scr[a, pl.ds(i, NE, stride=8), :], scr[a, pl.ds(4 + i, NE, stride=8), :]], axis=0)
                diag = jnp.where(col == 32 * i + r, x_i, diag)
                xb[a, :, T * i:T * i + T] = x_i.astype(BF)
            xb[a, :, 4 * T:5 * T] = jnp.where(row < NE, diag, 0.0).astype(BF)
            xb[a, :, 5 * T:] = jnp.where(row < NE, 0.0, diag).astype(BF)
        for n in range(3):
            cols = slice(256 * n, 256 * n + 256)
            gx = xb[0, :, cols]
            wx = xb[1, :, cols]
            gh = mm(fm[0], gx) + mm(fm[1], gx)
            wh = mm(fm[0], wx) + mm(fm[1], wx)
            pr = gh[:LEN] * wh[:LEN] - gh[LEN:] * wh[LEN:]
            pi = gh[:LEN] * wh[LEN:] + gh[LEN:] * wh[:LEN]
            prod = jnp.concatenate([pr, pi], axis=0)
            hi = prod.astype(BF)
            ph[:, cols] = hi
            pw[:, cols] = (prod - hi.astype(F32)).astype(BF)

        def back(cols):
            return mm(bm[0], ph[:, cols]) + mm(bm[1], ph[:, cols]) + mm(bm[0], pw[:, cols])

        y = back(slice(4 * T, 6 * T))
        fix = jnp.concatenate([-y[NE:, :T], y[NE:, T:]], axis=0)
        here = q_me < 32 if TILES[h][0][0] == TILES[h][0][1] else None
        for n in range(2):
            y = back(slice(256 * n, 256 * n + 256))
            for m in range(2):
                i = 2 * n + m
                z = y[:, T * m:T * m + T]
                if here is not None:
                    z = jnp.where((col == 32 * i + r) & here, fix, z)
                scr[0, pl.ds(i, NE, stride=8), :] = z[:NE]
                scr[0, pl.ds(4 + i, NE, stride=8), :] = z[NE:]
        ssend[h] = scr[0].reshape(NE, 8, T).astype(BF)

        @pl.loop(1, NE)
        def _(i):
            d = ring(i)
            away = lax.rem((1 - 2 * lo) * (lax.rem(lax.div(d, 4), 4) - zh) + 4, 4)
            far = lax.div(away, 2)
            kind = away + far * (5 - 2 * away)
            pltpu.make_async_remote_copy(
                src_ref=ssend.at[h, d], dst_ref=u_v.at[sp, h, q_me], send_sem=sgs.at[h], recv_sem=sgr.at[h, kind],
                device_id=(d, lax.rem(sp + 2 * far, 4)), device_id_type=MESH).start()

        pltpu.make_async_copy(ssend.at[h, me], u_v.at[sp, h, q_me], sgr.at[h, 0]).start()

    def part(k, h, z):
        return u_v.at[k, h, pl.ds(16 * z, 16)]

    def give(k, h, z, to, ss, rs):
        pltpu.make_async_remote_copy(
            src_ref=part(k, h, z), dst_ref=part(k, h, z), send_sem=ss, recv_sem=rs,
            device_id=(me, to), device_id_type=MESH).start()

    def whole(h, s):
        pltpu.make_async_copy(u_v.at[sp, h], u_v.at[sp, h], s).wait()

    first = ((sp, za), (sp, zb), (sp_z, zb), (sp_z, zc))
    second = ((sp_z, za), (sp_z, zd), (sp, zd), (sp, zc))

    def stage1(h, kinds=range(4)):
        for n in kinds:
            k, z = first[n]
            pltpu.make_async_copy(part(k, h, z), part(k, h, z), sgr.at[h, n]).wait()
            give(k, h, z, sp_z, zs.at[h], zr.at[h, n])
            give(k, h, z, sp_core, cs.at[0, h], cr.at[0, h])

    def stage2(h, kinds=range(4)):
        for n in kinds:
            k, z = second[n]
            pltpu.make_async_copy(part(k, h, z), part(k, h, z), zr.at[h, n]).wait()
            give(k, h, z, sp_core, cs.at[1, h], cr.at[1, h])

    def stage3(h):
        whole(h, cr.at[0, h])
        whole(h, cr.at[1, h])

    def tile(k, h, t):
        tmp[t] = u_v[k, h, 32 * t:32 * t + 32].astype(F32).reshape(2 * T, T)
        return [jnp.concatenate([tmp[t, pl.ds(4 * c + n, 32, stride=8), :] for n in range(4)], axis=0) for c in range(2)]

    def put(n, at, p):
        ur, ui = p[0].astype(BF), p[1].astype(BF)
        ue[n, at:at + T, 0:T] = ur
        ue[n, at:at + T, T:2 * T] = ui
        ue[n, at + T:at + 2 * T, 0:T] = -ui
        ue[n, at + T:at + 2 * T, T:2 * T] = ur

    def upper(p):
        return (jnp.where(row < col, p[0], 0.0),
                jnp.where(row < col, p[1], jnp.where(row == col, 0.5 * p[1], 0.0)))

    def lower(p):
        return (jnp.where(row > col, p[0], 0.0),
                jnp.where(row > col, p[1], jnp.where(row == col, 0.5 * p[0], 0.0)))

    def left(n, i, depth):
        return mm(rc[n, :, 2 * T * i:2 * T * (i + depth)], ue[n, 2 * T * i:2 * T * (i + depth), :])

    def place(n):
        return slice(2 * T * n, 2 * T * n + 2 * T)

    def rows01(n):
        put(n, 0, upper(tile(order[n], 0, 0)))
        lcat[:, place(n)] = left(n, 0, 1).astype(BF)
        put(n, 0, tile(order[n], 0, 1))
        put(n, 2 * T, lower(tile(order[n], 0, 0)))
        lcat[:, place(4 + n)] = left(n, 0, 2).astype(BF)

    def rows2(n):
        put(n, 0, tile(order[n], 1, 1))
        put(n, 2 * T, tile(order[n], 2, 0))
        put(n, 4 * T, upper(tile(order[n], 1, 0)))
        lcat[:, place(n)] = left(n, 0, 3).astype(BF)
        put(n, 4 * T, tile(order[n], 2, 1))
        put(n, 6 * T, lower(tile(order[n], 1, 0)))
        l3[n] = left(n, 2, 2)

    def rows3(n):
        put(n, 0, tile(order[n], 3, 0))
        put(n, 2 * T, tile(order[n], 3, 1))
        lcat[:, place(4 + n)] = (l3[n] + left(n, 0, 2)).astype(BF)

    def total(j, at, depth):
        k = slice(2 * T * at, 2 * T * (at + depth))
        c = slice(1024 * (j % 2) + 2 * T * at, 1024 * (j % 2) + 2 * T * (at + depth))
        for m in range(4):
            cols = slice(256 * m, 256 * m + 256)
            y = mm(lcat[:, c], rt[j, k, cols])
            half = slice(256 * (m % 2), 256 * (m % 2) + 256)
            x = (xr, xi)[m // 2]
            x[:, half] = y if j == 0 else x[:, half] + y

    def sigma_out(h):
        for t, (i, j) in enumerate(TILES[h]):
            pr, pi = tile(sp, h, t)
            prt = pr.T
            pit = pi.T
            a = slice(T * i, T * i + T)
            if i == j:
                b = slice(T * i + T, T * i + 2 * T)
                sig_ref[0, a, a] = jnp.where(row < col, pr, jnp.where(row > col, -prt, 0.0)).astype(BF)
                sig_ref[1, a, a] = jnp.where(row <= col, pi, pit).astype(BF)
                sig_ref[0, b, b] = jnp.where(row > col, pr, jnp.where(row < col, -prt, 0.0)).astype(BF)
                sig_ref[1, b, b] = jnp.where(row > col, pi, jnp.where(row < col, pit, pr)).astype(BF)
            else:
                b = slice(T * j, T * j + T)
                sig_ref[0, a, b] = pr.astype(BF)
                sig_ref[1, a, b] = pi.astype(BF)
                sig_ref[0, b, a] = (-prt).astype(BF)
                sig_ref[1, b, a] = pit.astype(BF)

    convolve(0)
    convolve(1)
    stage1(0, (0,))
    convolve(2)
    stage1(1, (0,))
    convolve(3)
    stage1(2, (0,))
    stage1(0, (1, 2, 3))
    stage1(1, (1, 2, 3))
    stage2(0)
    rows01(0)
    rows01(1)
    stage1(3, (0,))
    stage1(2, (1, 2, 3))
    stage2(1)
    sigma_out(0)
    sigma_out(1)
    stage3(0)
    rows01(2)
    rows01(3)
    total(0, 0, 4)
    stage1(3, (1, 2, 3))
    stage2(2)
    total(1, 0, 4)
    rows2(0)
    rows2(1)
    stage2(3)
    stage3(1)
    stage3(2)
    rows2(2)
    rows2(3)
    total(2, 0, 4)
    rows3(0)
    rows3(1)
    total(3, 0, 2)
    sigma_out(2)
    sigma_out(3)
    stage3(3)
    rows3(2)
    rows3(3)
    total(3, 2, 2)

    for h in range(CHUNKS):
        pltpu.make_async_copy(send.at[h, 0:NE - 1], send.at[h, 0:NE - 1], gws.at[h]).wait()
        pltpu.make_async_copy(ssend.at[h, 0:NE - 1], ssend.at[h, 0:NE - 1], sgs.at[h]).wait()
        whole(h, zs.at[h])
        whole(h, cs.at[0, h])
        whole(h, cs.at[1, h])


def results(sig_v, xr, xi, sig_ref, del_ref, out, sem):
    moves = [pltpu.make_async_copy(sig_v, sig_ref, sem.at[4])]
    moves[0].start()
    for i in range(4):
        a = slice(T * i, T * i + T)
        for j in range(i, 4):
            b = slice(T * j, T * j + T)
            dr = xr[a, b] - xr[b, a].T
            di = xi[a, b] + xi[b, a].T
            out[0, a, b] = dr.astype(BF)
            out[1, a, b] = di.astype(BF)
            if i != j:
                out[0, b, a] = (-dr.T).astype(BF)
                out[1, b, a] = di.T.astype(BF)
        moves.append(pltpu.make_async_copy(out.at[:, a, :], del_ref.at[:, a, :], sem.at[i]))
        moves[-1].start()
    for move in moves:
        move.wait()


def shards(g, w, r, idx):
    vmem = pl.BlockSpec(memory_space=pltpu.VMEM)
    hbm = pl.BlockSpec(memory_space=pltpu.HBM)
    out = jax.ShapeDtypeStruct((2, B, B), BF)
    dma = pltpu.SemaphoreType.DMA
    sig, xr, xi = pl.pallas_call(
        body,
        name="gw",
        out_shape=(out,) + (jax.ShapeDtypeStruct((B, B), F32),) * 2,
        in_specs=[hbm] * 4,
        out_specs=(vmem,) * 3,
        scratch_shapes=[
            pltpu.VMEM((2, B, B), BF),
            pltpu.VMEM((2, B, B), BF),
            pltpu.VMEM((1, NE), jnp.int32),
            pltpu.VMEM((4, B, 2 * B), BF),
            pltpu.VMEM((4, 2 * B, 2 * B), BF),
            pltpu.VMEM((CHUNKS, NE, 2, 8, T), BF),
            pltpu.VMEM((CHUNKS, NE, 2, 8, T), BF),
            pltpu.VMEM((CHUNKS, NE, 8, T), BF),
            pltpu.VMEM((4, CHUNKS, NE, 8, T), BF),
            pltpu.VMEM((2, 8 * NE, T), F32),
            pltpu.VMEM((2, 2 * T, T), F32),
            pltpu.VMEM((2, T, 6 * T), BF),
            pltpu.VMEM((2 * LEN, 6 * T), BF),
            pltpu.VMEM((2 * LEN, 6 * T), BF),
            pltpu.VMEM((2, 2 * LEN, T), BF),
            pltpu.VMEM((2, T, 2 * LEN), BF),
            pltpu.VMEM((4, 8 * T, 2 * T), BF),
            pltpu.VMEM((B, 4 * B), BF),
            pltpu.VMEM((4, B, 2 * T), F32),
            dma((6,)),
            dma((CHUNKS,)),
            dma((CHUNKS,)),
            dma((CHUNKS,)),
            dma((CHUNKS, 4)),
            dma((CHUNKS,)),
            dma((CHUNKS, 4)),
            dma((2, CHUNKS)),
            dma((2, CHUNKS)),
        ],
        compiler_params=pltpu.CompilerParams(collective_id=0, has_side_effects=True,
                                             vmem_limit_bytes=50 * 1024 * 1024),
    )(g.reshape(2, B, B), w.reshape(2, B, B), r.reshape(8, B, B), idx.reshape(1, NE))
    sig, delta = pl.pallas_call(
        results,
        name="results",
        out_shape=(out, out),
        in_specs=[vmem] * 3,
        out_specs=(pl.BlockSpec(memory_space=pl.ANY),) * 2,
        scratch_shapes=[pltpu.VMEM((2, B, B), BF), dma((5,))],
        compiler_params=pltpu.CompilerParams(vmem_limit_bytes=16 * 1024 * 1024),
    )(sig, xr, xi)
    return sig.reshape(1, 2, 1, B, B), delta.reshape(1, 2, 1, B, B)


def solution(mesh):
    block = P("energy", None, "space", None, None)
    return jax.shard_map(
        shards,
        mesh=mesh,
        in_specs=(block, block, P("energy", None, "space", None, None, None), P()),
        out_specs=(block, block),
        check_vma=False,
    )
```

```python
import math

import jax
import jax.numpy as jnp
from jax import lax
from jax.experimental import pallas as pl
from jax.experimental.pallas import tpu as pltpu
from jax.sharding import PartitionSpec as P

MESH = pl.DeviceIdType.MESH
NE = 64
B = 512
T = 128
LEN = 96
TILES = (((0, 0), (0, 1)), ((2, 2), (0, 2)), ((1, 2), (2, 3)), ((0, 3), (1, 3)))
CHUNKS = len(TILES)
BF = jnp.bfloat16
F32 = jnp.float32


def mm(a, b):
    return jnp.dot(a, b, preferred_element_type=F32)


def body(g_hbm, w_hbm, r_hbm, idx_hbm, sig_ref, xr, xi,
         g_v, w_v, idx_v, rc, rt, send, recv, ssend, u_v, scr, tmp,
         xb, ph, pw, fm, bm, ue, lcat, l2, l3,
         lsem, gws, gwr, sgs, sgr, zs, zr, cs, cr):
    me = lax.axis_index("energy")
    sp = lax.axis_index("space")
    lo = sp // 2
    sp_core = lo * 2 + (sp + 1) % 2
    sp_z = (sp + 2) % 4
    sp_zc = (sp_core + 2) % 4
    order = (sp, sp_z, sp_core, sp_zc)
    zh = me // 4 % 4
    q_me = zh * 16 + me // 16 * 4 + me % 4
    za = zh
    zb = (zh + 3 + 2 * lo) % 4
    zc = (zh + 2) % 4
    zd = (zh + 1 + 2 * lo) % 4

    def ring(i):
        return lax.rem(me + i, NE)

    barrier = pltpu.get_barrier_semaphore()

    @pl.loop(1, NE)
    def _(i):
        pl.semaphore_signal(barrier, inc=1, device_id=(ring(i), sp), device_id_type=MESH)

    pl.semaphore_signal(barrier, inc=1, device_id=(me, sp_core), device_id_type=MESH)
    pl.semaphore_signal(barrier, inc=1, device_id=(me, sp_z), device_id_type=MESH)

    def tiles_of(h):
        for i, j in TILES[h]:
            for k in range(2 if i == j else 1):
                yield i + k, j + k

    def load(h, src, dst, i, j):
        at = (slice(None), slice(T * i, T * i + T), slice(T * j, T * j + T))
        return pltpu.make_async_copy(src.at[at], dst.at[at], lsem.at[h])

    for h in range(CHUNKS):
        for i, j in tiles_of(h):
            load(h, g_hbm, g_v, i, j).start()
            load(h, w_hbm, w_v, i, j).start()

    row = lax.broadcasted_iota(jnp.int32, (T, T), 0)
    col = lax.broadcasted_iota(jnp.int32, (T, T), 1)
    for h in range(CHUNKS):
        n_tiles = len(list(tiles_of(h)))
        all_of = g_v.at[:, 0:2 * T, 0:T * n_tiles]
        pltpu.make_async_copy(all_of, all_of, lsem.at[h]).wait()
        for t, (i, j) in enumerate(TILES[h]):
            for a, src in enumerate((g_v, w_v)):
                if i == j:
                    k = i + 1
                    d0r, d0i = (src[c, T * i:T * i + T, T * i:T * i + T].astype(F32) for c in range(2))
                    d1r, d1i = (src[c, T * k:T * k + T, T * k:T * k + T].astype(F32) for c in range(2))
                    both = (jnp.where(row < col, d0r, jnp.where(row > col, d1r, d1i)), jnp.where(row <= col, d0i, d1i))
                else:
                    both = [src[c, T * i:T * i + T, T * j:T * j + T].astype(F32) for c in range(2)]
                for c in range(2):
                    for n in range(4):
                        tmp[a, pl.ds(c * 4 + n, 32, stride=8), :] = both[c][32 * n:32 * n + 32]
                send[h, 32 * t:32 * t + 32, a] = tmp[a].reshape(32, 8, T).astype(BF)

        if h == 0:
            pl.semaphore_wait(barrier, NE + 1)

        @pl.loop(1, NE)
        def _(i):
            d = ring(i)
            q = lax.rem(lax.div(d, 4), 4) * 16 + lax.div(d, 16) * 4 + lax.rem(d, 4)
            pltpu.make_async_remote_copy(
                src_ref=send.at[h, q], dst_ref=recv.at[h, me], send_sem=gws.at[h], recv_sem=gwr.at[h],
                device_id=(d, sp), device_id_type=MESH).start()

        pltpu.make_async_copy(send.at[h, q_me], recv.at[h, me], gwr.at[h]).start()

    small = pltpu.make_async_copy(idx_hbm, idx_v, lsem.at[5])
    small.start()
    for n, k in enumerate(order):
        for c in range(2):
            for i in range(4):
                pltpu.make_async_copy(r_hbm.at[4 * c + k, :, T * i:T * i + T],
                                      rc.at[n, :, T * (2 * i + c):T * (2 * i + c) + T], lsem.at[4]).start()

    small.wait()

    def lines(shape, axis):
        return lax.broadcasted_iota(jnp.int32, shape, axis)

    twice = (lines((NE, T), 0) == lines((NE, T), 1) % NE).astype(F32).astype(BF)
    point = mm(jnp.broadcast_to(idx_v[...].astype(F32), (8, NE)).astype(BF), twice)[0:1, :]
    wide = (2 * LEN, T)
    out_c = (lines(wide, 0) >= LEN).astype(F32)
    freq = lines(wide, 0).astype(F32) - LEN * out_c
    in_c = (lines(wide, 1) >= NE).astype(F32)

    def wave(steps):
        turns = steps - LEN * jnp.floor((steps + 0.5) / LEN)
        return jnp.cos(turns * (2.0 * math.pi / LEN))

    def halves(m):
        high = m.astype(BF)
        return high, (m - high.astype(F32)).astype(BF)

    quarter = LEN // 4
    eye = (lines((2 * LEN, 2 * LEN), 0) == lines((2 * LEN, 2 * LEN), 1)).astype(F32).astype(BF)
    for a, m in enumerate(halves(wave(freq * point + quarter * (out_c - in_c)))):
        fm[a] = m
    for a, m in enumerate(halves(wave(freq * (point + NE // 2) + quarter * (1.0 - in_c + out_c)) * (NE**-0.5 / LEN))):
        bm[a] = lax.dot_general(m, eye, (((0,), (0,)), ((), ())), preferred_element_type=F32).astype(BF)

    pltpu.make_async_copy(rc, rc, lsem.at[4]).wait()

    @pl.loop(0, 4)
    def _(n):
        at = pl.multiple_of(n * 2 * T, 2 * T)
        for j in range(4):
            for i in range(4):
                r_t = rc[n, T * i:T * i + T, 2 * T * j:2 * T * j + T].astype(F32).T
                i_t = rc[n, T * i:T * i + T, 2 * T * j + T:2 * T * j + 2 * T].astype(F32).T
                rt[j, pl.ds(at, T), T * i:T * i + T] = r_t.astype(BF)
                rt[j, pl.ds(at, T), B + T * i:B + T * i + T] = (-i_t).astype(BF)
                rt[j, pl.ds(at + T, T), T * i:T * i + T] = i_t.astype(BF)
                rt[j, pl.ds(at + T, T), B + T * i:B + T * i + T] = r_t.astype(BF)

    def convolve(h):
        pltpu.make_async_copy(recv.at[h], recv.at[h], gwr.at[h]).wait()
        for a in range(2):
            scr[a] = recv[h, :, a].astype(F32).reshape(8 * NE, T)
        r = q_me % 32
        for a in range(2):
            diag = jnp.zeros((T, T), F32)
            for i in range(4):
                x_i = jnp.concatenate(
                    [scr[a, pl.ds(i, NE, stride=8), :], scr[a, pl.ds(4 + i, NE, stride=8), :]], axis=0)
                diag = jnp.where(col == 32 * i + r, x_i, diag)
                xb[a, :, T * i:T * i + T] = x_i.astype(BF)
            xb[a, :, 4 * T:5 * T] = jnp.where(row < NE, diag, 0.0).astype(BF)
            xb[a, :, 5 * T:] = jnp.where(row < NE, 0.0, diag).astype(BF)
        for n in range(3):
            cols = slice(256 * n, 256 * n + 256)
            gx = xb[0, :, cols]
            wx = xb[1, :, cols]
            gh = mm(fm[0], gx) + mm(fm[1], gx)
            wh = mm(fm[0], wx) + mm(fm[1], wx)
            pr = gh[:LEN] * wh[:LEN] - gh[LEN:] * wh[LEN:]
            pi = gh[:LEN] * wh[LEN:] + gh[LEN:] * wh[:LEN]
            prod = jnp.concatenate([pr, pi], axis=0)
            hi = prod.astype(BF)
            ph[:, cols] = hi
            pw[:, cols] = (prod - hi.astype(F32)).astype(BF)

        def back(cols):
            return mm(bm[0], ph[:, cols]) + mm(bm[1], ph[:, cols]) + mm(bm[0], pw[:, cols])

        y = back(slice(4 * T, 6 * T))
        fix = jnp.concatenate([-y[NE:, :T], y[NE:, T:]], axis=0)
        here = q_me < 32 if TILES[h][0][0] == TILES[h][0][1] else None
        for n in range(2):
            y = back(slice(256 * n, 256 * n + 256))
            for m in range(2):
                i = 2 * n + m
                z = y[:, T * m:T * m + T]
                if here is not None:
                    z = jnp.where((col == 32 * i + r) & here, fix, z)
                scr[0, pl.ds(i, NE, stride=8), :] = z[:NE]
                scr[0, pl.ds(4 + i, NE, stride=8), :] = z[NE:]
        ssend[h] = scr[0].reshape(NE, 8, T).astype(BF)

        @pl.loop(1, NE)
        def _(i):
            d = ring(i)
            away = lax.rem((1 - 2 * lo) * (lax.rem(lax.div(d, 4), 4) - zh) + 4, 4)
            far = lax.div(away, 2)
            kind = away + far * (5 - 2 * away)
            pltpu.make_async_remote_copy(
                src_ref=ssend.at[h, d], dst_ref=u_v.at[sp, h, q_me], send_sem=sgs.at[h], recv_sem=sgr.at[h, kind],
                device_id=(d, lax.rem(sp + 2 * far, 4)), device_id_type=MESH).start()

        pltpu.make_async_copy(ssend.at[h, me], u_v.at[sp, h, q_me], sgr.at[h, 0]).start()

    def part(k, h, z):
        return u_v.at[k, h, pl.ds(16 * z, 16)]

    def give(k, h, z, to, ss, rs):
        pltpu.make_async_remote_copy(
            src_ref=part(k, h, z), dst_ref=part(k, h, z), send_sem=ss, recv_sem=rs,
            device_id=(me, to), device_id_type=MESH).start()

    def whole(h, s):
        pltpu.make_async_copy(u_v.at[sp, h], u_v.at[sp, h], s).wait()

    first = ((sp, za), (sp, zb), (sp_z, zb), (sp_z, zc))
    second = ((sp_z, za), (sp_z, zd), (sp, zd), (sp, zc))

    def stage1(h, kinds=range(4)):
        for n in kinds:
            k, z = first[n]
            pltpu.make_async_copy(part(k, h, z), part(k, h, z), sgr.at[h, n]).wait()
            give(k, h, z, sp_z, zs.at[h], zr.at[h, n])
            give(k, h, z, sp_core, cs.at[0, h], cr.at[0, h])

    def stage2(h, kinds=range(4)):
        for n in kinds:
            k, z = second[n]
            pltpu.make_async_copy(part(k, h, z), part(k, h, z), zr.at[h, n]).wait()
            give(k, h, z, sp_core, cs.at[1, h], cr.at[1, h])

    def stage3(h):
        whole(h, cr.at[0, h])
        whole(h, cr.at[1, h])

    def tile(k, h, t):
        tmp[t] = u_v[k, h, 32 * t:32 * t + 32].astype(F32).reshape(2 * T, T)
        return [jnp.concatenate([tmp[t, pl.ds(4 * c + n, 32, stride=8), :] for n in range(4)], axis=0) for c in range(2)]

    def put(n, at, p):
        ur, ui = p[0].astype(BF), p[1].astype(BF)
        ue[n, at:at + T, 0:T] = ur
        ue[n, at:at + T, T:2 * T] = ui
        ue[n, at + T:at + 2 * T, 0:T] = -ui
        ue[n, at + T:at + 2 * T, T:2 * T] = ur

    def upper(p):
        return (jnp.where(row < col, p[0], 0.0),
                jnp.where(row < col, p[1], jnp.where(row == col, 0.5 * p[1], 0.0)))

    def lower(p):
        return (jnp.where(row > col, p[0], 0.0),
                jnp.where(row > col, p[1], jnp.where(row == col, 0.5 * p[0], 0.0)))

    def left(n, i, depth):
        return mm(rc[n, :, 2 * T * i:2 * T * (i + depth)], ue[n, 2 * T * i:2 * T * (i + depth), :])

    def place(n):
        return slice(2 * T * n, 2 * T * n + 2 * T)

    def rows01(n):
        put(n, 0, upper(tile(order[n], 0, 0)))
        lcat[:, place(n)] = left(n, 0, 1).astype(BF)
        put(n, 0, tile(order[n], 0, 1))
        put(n, 2 * T, lower(tile(order[n], 0, 0)))
        lcat[:, place(4 + n)] = left(n, 0, 2).astype(BF)

    def rows2_early(n):
        d = tile(order[n], 1, 0)
        put(n, 0, tile(order[n], 1, 1))
        put(n, 4 * T, upper(d))
        put(n, 6 * T, lower(d))
        l2[n] = left(n, 0, 1) + left(n, 2, 1)
        l3[n] = left(n, 3, 1)

    def rows2(n):
        put(n, 2 * T, tile(order[n], 2, 0))
        put(n, 4 * T, tile(order[n], 2, 1))
        lcat[:, place(n)] = (l2[n] + left(n, 1, 1)).astype(BF)
        l3[n] += left(n, 2, 1)

    def rows3(n):
        put(n, 0, tile(order[n], 3, 0))
        put(n, 2 * T, tile(order[n], 3, 1))
        lcat[:, place(4 + n)] = (l3[n] + left(n, 0, 2)).astype(BF)

    def total(j, at, depth):
        k = slice(2 * T * at, 2 * T * (at + depth))
        c = slice(1024 * (j % 2) + 2 * T * at, 1024 * (j % 2) + 2 * T * (at + depth))
        for m in range(4):
            cols = slice(256 * m, 256 * m + 256)
            y = mm(lcat[:, c], rt[j, k, cols])
            half = slice(256 * (m % 2), 256 * (m % 2) + 256)
            x = (xr, xi)[m // 2]
            x[:, half] = y if j == 0 else x[:, half] + y

    def sigma_out(h):
        for t, (i, j) in enumerate(TILES[h]):
            pr, pi = tile(sp, h, t)
            prt = pr.T
            pit = pi.T
            a = slice(T * i, T * i + T)
            if i == j:
                b = slice(T * i + T, T * i + 2 * T)
                sig_ref[0, a, a] = jnp.where(row < col, pr, jnp.where(row > col, -prt, 0.0)).astype(BF)
                sig_ref[1, a, a] = jnp.where(row <= col, pi, pit).astype(BF)
                sig_ref[0, b, b] = jnp.where(row > col, pr, jnp.where(row < col, -prt, 0.0)).astype(BF)
                sig_ref[1, b, b] = jnp.where(row > col, pi, jnp.where(row < col, pit, pr)).astype(BF)
            else:
                b = slice(T * j, T * j + T)
                sig_ref[0, a, b] = pr.astype(BF)
                sig_ref[1, a, b] = pi.astype(BF)
                sig_ref[0, b, a] = (-prt).astype(BF)
                sig_ref[1, b, a] = pit.astype(BF)

    convolve(0)
    convolve(1)
    stage1(0, (0,))
    convolve(2)
    stage1(1, (0,))
    convolve(3)
    stage1(2, (0,))
    stage1(0, (1, 2, 3))
    stage1(1, (1, 2, 3))
    stage2(0)
    rows01(0)
    rows01(1)
    stage1(3, (0,))
    stage1(2, (1, 2, 3))
    stage2(1)
    sigma_out(0)
    sigma_out(1)
    stage3(0)
    rows01(2)
    rows01(3)
    rows2_early(0)
    rows2_early(1)
    total(0, 0, 4)
    stage1(3, (1, 2, 3))
    stage2(2)
    total(1, 0, 4)
    stage3(1)
    rows2_early(2)
    rows2_early(3)
    rows2(0)
    rows2(1)
    stage2(3)
    stage3(2)
    rows2(2)
    rows2(3)
    total(2, 0, 4)
    rows3(0)
    rows3(1)
    total(3, 0, 2)
    sigma_out(2)
    sigma_out(3)
    stage3(3)
    rows3(2)
    rows3(3)
    total(3, 2, 2)

    for h in range(CHUNKS):
        pltpu.make_async_copy(send.at[h, 0:NE - 1], send.at[h, 0:NE - 1], gws.at[h]).wait()
        pltpu.make_async_copy(ssend.at[h, 0:NE - 1], ssend.at[h, 0:NE - 1], sgs.at[h]).wait()
        whole(h, zs.at[h])
        whole(h, cs.at[0, h])
        whole(h, cs.at[1, h])


def results(sig_v, xr, xi, sig_ref, del_ref, out, sem):
    moves = [pltpu.make_async_copy(sig_v, sig_ref, sem.at[4])]
    moves[0].start()
    for i in range(4):
        a = slice(T * i, T * i + T)
        for j in range(i, 4):
            b = slice(T * j, T * j + T)
            dr = xr[a, b] - xr[b, a].T
            di = xi[a, b] + xi[b, a].T
            out[0, a, b] = dr.astype(BF)
            out[1, a, b] = di.astype(BF)
            if i != j:
                out[0, b, a] = (-dr.T).astype(BF)
                out[1, b, a] = di.T.astype(BF)
        moves.append(pltpu.make_async_copy(out.at[:, a, :], del_ref.at[:, a, :], sem.at[i]))
        moves[-1].start()
    for move in moves:
        move.wait()


def shards(g, w, r, idx):
    vmem = pl.BlockSpec(memory_space=pltpu.VMEM)
    hbm = pl.BlockSpec(memory_space=pltpu.HBM)
    out = jax.ShapeDtypeStruct((2, B, B), BF)
    dma = pltpu.SemaphoreType.DMA
    sig, xr, xi = pl.pallas_call(
        body,
        name="gw",
        out_shape=(out,) + (jax.ShapeDtypeStruct((B, B), F32),) * 2,
        in_specs=[hbm] * 4,
        out_specs=(vmem,) * 3,
        scratch_shapes=[
            pltpu.VMEM((2, B, B), BF),
            pltpu.VMEM((2, B, B), BF),
            pltpu.VMEM((1, NE), jnp.int32),
            pltpu.VMEM((4, B, 2 * B), BF),
            pltpu.VMEM((4, 2 * B, 2 * B), BF),
            pltpu.VMEM((CHUNKS, NE, 2, 8, T), BF),
            pltpu.VMEM((CHUNKS, NE, 2, 8, T), BF),
            pltpu.VMEM((CHUNKS, NE, 8, T), BF),
            pltpu.VMEM((4, CHUNKS, NE, 8, T), BF),
            pltpu.VMEM((2, 8 * NE, T), F32),
            pltpu.VMEM((2, 2 * T, T), F32),
            pltpu.VMEM((2, T, 6 * T), BF),
            pltpu.VMEM((2 * LEN, 6 * T), BF),
            pltpu.VMEM((2 * LEN, 6 * T), BF),
            pltpu.VMEM((2, 2 * LEN, T), BF),
            pltpu.VMEM((2, T, 2 * LEN), BF),
            pltpu.VMEM((4, 8 * T, 2 * T), BF),
            pltpu.VMEM((B, 4 * B), BF),
            pltpu.VMEM((4, B, 2 * T), F32),
            pltpu.VMEM((4, B, 2 * T), F32),
            dma((6,)),
            dma((CHUNKS,)),
            dma((CHUNKS,)),
            dma((CHUNKS,)),
            dma((CHUNKS, 4)),
            dma((CHUNKS,)),
            dma((CHUNKS, 4)),
            dma((2, CHUNKS)),
            dma((2, CHUNKS)),
        ],
        compiler_params=pltpu.CompilerParams(collective_id=0, has_side_effects=True,
                                             vmem_limit_bytes=50 * 1024 * 1024),
    )(g.reshape(2, B, B), w.reshape(2, B, B), r.reshape(8, B, B), idx.reshape(1, NE))
    sig, delta = pl.pallas_call(
        results,
        name="results",
        out_shape=(out, out),
        in_specs=[vmem] * 3,
        out_specs=(pl.BlockSpec(memory_space=pl.ANY),) * 2,
        scratch_shapes=[pltpu.VMEM((2, B, B), BF), dma((5,))],
        compiler_params=pltpu.CompilerParams(vmem_limit_bytes=16 * 1024 * 1024),
    )(sig, xr, xi)
    return sig.reshape(1, 2, 1, B, B), delta.reshape(1, 2, 1, B, B)


def solution(mesh):
    block = P("energy", None, "space", None, None)
    return jax.shard_map(
        shards,
        mesh=mesh,
        in_specs=(block, block, P("energy", None, "space", None, None, None), P()),
        out_specs=(block, block),
        check_vma=False,
    )
```
